32 devices in a mesh: dp: 8 (over z, y), tensor: 4 (over x, core).
Axes of the slice: x: 2, y: 2, z: 4, core: 2. Of those that a mesh axis runs over, the one named last changes fastest.
Arguments:
- tokens: float32 [4096, 1152], P(('dp', 'tensor')), may hold values from -6 to 6
- timesteps: int32 [16], replicated, may hold values from 0 to 999
- labels: int32 [16], replicated, may hold values from 0 to 1000
- time_weight: float32 [256, 1152], P(None, 'dp'), may hold values from -0.5 to 0.5
- class_table: float32 [1001, 1152], P(None, 'dp'), may hold values from -6 to 6
- mod_weight: bfloat16 [1, 1152, 6912], P(None, 'dp', 'tensor'), may hold values from -0.1875 to 0.1875
- mod_bias: float32 [1, 6912], replicated, may hold values from -3 to 3
- qkv_weight: bfloat16 [1, 3, 1152, 1152], P(None, None, 'dp', 'tensor'), may hold values from -0.1875 to 0.1875
- qv_bias: float32 [1, 2, 1152], replicated, may hold values from -3 to 3
- proj_weight: bfloat16 [1, 1152, 1152], P(None, 'tensor', 'dp'), may hold values from -1.25 to 1.25
- proj_bias: float32 [1, 1152], replicated, may hold values from -3 to 3
- up_weight: bfloat16 [1, 1152, 4608], P(None, 'dp', 'tensor'), may hold values from -0.1875 to 0.1875
- up_bias: float32 [1, 4608], replicated, may hold values from -3 to 3
- down_weight: bfloat16 [1, 4608, 1152], P(None, 'tensor', 'dp'), may hold values from -0.125 to 0.125
- down_bias: float32 [1, 1152], replicated, may hold values from -3 to 3
- grad_output: float32 [4096, 1152], P(('dp', 'tensor')), may hold values from -6 to 6
Outputs:
- output: float32 [4096, 1152], P(('dp', 'tensor'))
- grad_tokens: float32 [4096, 1152], P(('dp', 'tensor'))
- grad_time_weight: float32 [256, 1152], P(None, 'dp')
- grad_class_table: float32 [1001, 1152], P(None, 'dp')
- grad_mod_weight: float32 [1, 1152, 6912], P(None, 'dp', 'tensor')
- grad_mod_bias: float32 [1, 6912], replicated
- grad_qkv_weight: float32 [1, 3, 1152, 1152], P(None, None, 'dp', 'tensor')
- grad_qv_bias: float32 [1, 2, 1152], replicated
- grad_proj_weight: float32 [1, 1152, 1152], P(None, 'tensor', 'dp')
- grad_proj_bias: float32 [1, 1152], replicated
- grad_up_weight: float32 [1, 1152, 4608], P(None, 'dp', 'tensor')
- grad_up_bias: float32 [1, 4608], replicated
- grad_down_weight: float32 [1, 4608, 1152], P(None, 'tensor', 'dp')
- grad_down_bias: float32 [1, 1152], replicated
The draws below stay inside these ranges and needn't reach their ends.
All inputs are finite; a program needn't handle non-finite values.
Results may differ from the reference program's by a relative error of at most 0.025.
Values may be sent and summed in bfloat16 or wider, within the bound.
A program may use at most 128 MiB of HBM per device.

```python
import math
import jax
import jax.numpy as jnp
from jax import lax

D = 1152
HEADS = 16
HEAD_DIM = 72
FF = 4608
FREQ = 256
CLASSES = 1001
SEQ = 256
LAYERS = 1
LAT_DEV = 2
LATENTS = 16
TOKENS = 4096
N_TENSOR = 4


def place_ends(entries, stream_key, smallest, high):
    spot = [jax.random.randint(jax.random.fold_in(stream_key, axis), (), 0, length) for axis, length in enumerate(entries.shape)]
    longest = entries.shape.index(max(entries.shape))
    beside = spot[:longest] + [(spot[longest] + 1) % entries.shape[longest]] + spot[longest + 1:]
    return entries.at[tuple(spot)].set(smallest).at[tuple(beside)].set(high)


def raised(values, rng, source, target, shards_of, factor):
    def block_of(dim):
        return (jnp.arange(values.shape[dim]) // (values.shape[dim] // shards_of)).reshape((-1,) + (1,) * (values.ndim - 1 - dim))

    one_side = jax.random.permutation(rng, shards_of)[block_of(target)]
    second = (block_of(target) + shards_of // 2) % shards_of
    return jnp.where((block_of(source) == one_side) | (block_of(source) == second), factor * values, values)


def block_scale(rng, extent, shards, least, high):
    gain = 1.0
    for dim, blocks in shards:
        steps = jax.random.uniform(jax.random.fold_in(jax.random.fold_in(rng, 6), dim), (blocks,), jnp.float32, least / len(shards), high / len(shards))
        gain = gain * jnp.repeat(jnp.exp(steps), extent[dim] // blocks).reshape((-1,) + (1,) * (len(extent) - 1 - dim))
    return gain


def normal_values(key, dims, deviation, limit, cuts=(), kind=jnp.bfloat16):
    factor_of = block_scale(key, dims, cuts, -0.22, 0.18) if cuts else 1.0
    values = jax.random.normal(key, dims, jnp.float32) * deviation * factor_of
    return jnp.minimum(jnp.maximum(values, -limit), limit).astype(kind)


def noise_with(rng, shape, scale, most, cuts, heavy, kind=jnp.bfloat16):
    drawn = scale * jax.random.normal(rng, shape, jnp.float32)
    if cuts:
        drawn = drawn * block_scale(rng, shape, cuts, -0.22, 0.18)
    return jnp.clip(raised(drawn, jax.random.fold_in(rng, 3), *heavy), -most, most).astype(kind)


def setup_inputs(seed: int = 0) -> dict:
    arg_keys = jax.random.split(jax.random.key(seed), 17)
    return {
        "tokens": normal_values(arg_keys[0], (TOKENS, D), 1.0, 6.0, ((0, 32),), jnp.float32),
        "timesteps": place_ends(jax.random.randint(arg_keys[1], (LATENTS,), 0, 1000), jax.random.fold_in(arg_keys[1], 1), 0, 999).astype(jnp.int32),
        "labels": place_ends(jax.random.randint(arg_keys[2], (LATENTS,), 0, CLASSES), jax.random.fold_in(arg_keys[2], 1), 0, CLASSES - 1).astype(jnp.int32),
        "time_weight": normal_values(arg_keys[3], (FREQ, D), (FREQ // 2) ** -0.5, 0.5, ((1, 8),), jnp.float32),
        "class_table": normal_values(arg_keys[4], (CLASSES, D), 1.0, 6.0, ((1, 8),), jnp.float32),
        "mod_weight": normal_values(arg_keys[5], (LAYERS, D, 6 * D), D ** -0.5, 0.1875, ((1, 8), (2, 4))),
        "mod_bias": normal_values(arg_keys[6], (LAYERS, 6 * D), 0.5, 3.0, (), jnp.float32),
        "qkv_weight": normal_values(arg_keys[7], (LAYERS, 3, D, D), D ** -0.5, 0.1875, ((2, 8), (3, 4))),
        "qv_bias": normal_values(arg_keys[8], (LAYERS, 2, D), 0.5, 3.0, (), jnp.float32),
        "proj_weight": normal_values(arg_keys[9], (LAYERS, D, D), (max(D // 48, 8)) ** -0.5, 1.25, ((1, 4), (2, 8))),
        "proj_bias": normal_values(arg_keys[10], (LAYERS, D), 0.5, 3.0, (), jnp.float32),
        "up_weight": normal_values(arg_keys[11], (LAYERS, D, FF), D ** -0.5, 0.1875, ((1, 8), (2, 4))),
        "up_bias": normal_values(arg_keys[12], (LAYERS, FF), 0.5, 3.0, (), jnp.float32),
        "down_weight": normal_values(arg_keys[13], (LAYERS, FF, D), (FF // 2) ** -0.5, 0.125, ((1, 4), (2, 8))),
        "down_bias": normal_values(arg_keys[14], (LAYERS, D), 0.5, 3.0, (), jnp.float32),
        "grad_output": noise_with(arg_keys[15], (TOKENS, D), 1.0, 6.0, ((0, 32),), (0, 1, 32, 2.75), jnp.float32),
    }


EPSILON = 1e-06
PRECISE = lax.Precision.HIGHEST
GELU_COEFF = math.sqrt(2.0 / math.pi)
CUBIC_COEFF = 0.044715

def widen(values):
    return lax.optimization_barrier(values).astype(jnp.float32)

def time_features(timesteps, width):
    half_width = width // 2
    freq_rates = jnp.exp(-math.log(10000.0) * jnp.arange(half_width, dtype=jnp.float32) / half_width)
    angles = timesteps.astype(jnp.float32)[:, None] * freq_rates[None, :]
    return jnp.concatenate([jnp.cos(angles), jnp.sin(angles)], axis=1)

def layer_norm(values):
    average = lax.optimization_barrier(jnp.mean(values, axis=-1, keepdims=True))
    centred = values - average
    inverse = lax.rsqrt(lax.optimization_barrier(jnp.mean(centred * centred, axis=-1, keepdims=True)) + EPSILON)
    return (centred * inverse, inverse)

def norm_back(normed, inverse, grad_normed):
    first = lax.optimization_barrier(jnp.mean(grad_normed, axis=-1, keepdims=True))
    second = lax.optimization_barrier(jnp.mean(grad_normed * normed, axis=-1, keepdims=True))
    return inverse * (grad_normed - first - normed * second)

def gelu_value(values):
    return 0.5 * values * (1.0 + jnp.tanh(GELU_COEFF * (values + CUBIC_COEFF * values * values * values)))

def gelu_slope(values):
    tangent = jnp.tanh(GELU_COEFF * (values + CUBIC_COEFF * values * values * values))
    return 0.5 * (1.0 + tangent) + 0.5 * values * (1.0 - tangent * tangent) * GELU_COEFF * (1.0 + 3.0 * CUBIC_COEFF * values * values)

def silu_slope(values):
    logistic = jax.nn.sigmoid(values)
    return logistic * (1.0 + values * (1.0 - logistic))

def split_heads(values, latent_count):
    return values.reshape(latent_count, SEQ, HEADS, HEAD_DIM)

def group_sum(lefts, weights):
    width = lefts[0].shape[1] // N_TENSOR
    total = None
    for group in range(N_TENSOR):
        part = None
        for left, weight in zip(lefts, weights):
            term = jnp.dot(left[:, group * width:(group + 1) * width], weight[:, group * width:(group + 1) * width].T, preferred_element_type=jnp.float32)
            part = term if part is None else part + term
        rounded = widen(part.astype(jnp.bfloat16))
        total = rounded if total is None else total + rounded
    return total

def block_pass(inputs, grad_rows, mod_rows, weights):
    qkv_weight, qv_bias, proj_weight, proj_bias, up_weight, up_bias, down_weight, down_bias = weights
    latent_count = inputs.shape[0]
    all_rows = latent_count * SEQ
    score_scale = 1.0 / math.sqrt(HEAD_DIM)
    stored = []
    current_x = inputs
    for current in range(LAYERS):
        pieces = [mod_rows[current][:, None, segment * D:(segment + 1) * D] for segment in range(6)]
        shift_attn, scale_attn, gate_attn, shift_mlp, scale_mlp, gate_mlp = pieces
        normed_attn, inverse_attn = layer_norm(current_x)
        attn_in = (normed_attn * (1.0 + scale_attn) + shift_attn).astype(jnp.bfloat16).reshape(all_rows, D)
        queries = (jnp.dot(attn_in, qkv_weight[current, 0], preferred_element_type=jnp.float32) + qv_bias[current, 0]).astype(jnp.bfloat16)
        key_rows = jnp.dot(attn_in, qkv_weight[current, 1], preferred_element_type=jnp.float32).astype(jnp.bfloat16)
        value_rows = (jnp.dot(attn_in, qkv_weight[current, 2], preferred_element_type=jnp.float32) + qv_bias[current, 1]).astype(jnp.bfloat16)
        scores = jnp.einsum('bqhd,bkhd->bhqk', widen(split_heads(queries, latent_count)), widen(split_heads(key_rows, latent_count))) * score_scale
        log_total = jnp.log(lax.optimization_barrier(jnp.sum(jnp.exp(scores), axis=-1, keepdims=True)))
        prob_low = jnp.exp(scores - log_total).astype(jnp.bfloat16)
        attended = jnp.einsum('bhqk,bkhd->bqhd', widen(prob_low), widen(split_heads(value_rows, latent_count))).astype(jnp.bfloat16).reshape(all_rows, D)
        attn_out = (jnp.dot(attended, proj_weight[current], preferred_element_type=jnp.float32) + proj_bias[current]).reshape(latent_count, SEQ, D)
        middle = current_x + gate_attn * attn_out
        normed_mlp, inverse_mlp = layer_norm(middle)
        mlp_in = (normed_mlp * (1.0 + scale_mlp) + shift_mlp).astype(jnp.bfloat16).reshape(all_rows, D)
        pre_act = jnp.dot(mlp_in, up_weight[current], preferred_element_type=jnp.float32) + up_bias[current]
        gelu_low = gelu_value(pre_act).astype(jnp.bfloat16)
        mlp_out = (jnp.dot(gelu_low, down_weight[current], preferred_element_type=jnp.float32) + down_bias[current]).reshape(latent_count, SEQ, D)
        stored.append((normed_attn, inverse_attn, attn_in, queries, key_rows, value_rows, log_total, attended, attn_out, normed_mlp, inverse_mlp, mlp_in, pre_act, gelu_low, mlp_out))
        current_x = middle + gate_mlp * mlp_out
    grad_x = grad_rows
    mod_grads = [None] * LAYERS
    layer_grads = [None] * LAYERS
    for current in reversed(range(LAYERS)):
        normed_attn, inverse_attn, attn_in, queries, key_rows, value_rows, log_total, attended, attn_out, normed_mlp, inverse_mlp, mlp_in, pre_act, gelu_low, mlp_out = stored[current]
        pieces = [mod_rows[current][:, None, segment * D:(segment + 1) * D] for segment in range(6)]
        shift_attn, scale_attn, gate_attn, shift_mlp, scale_mlp, gate_mlp = pieces
        d_mlp = grad_x * gate_mlp
        d_gate_mlp = lax.optimization_barrier(jnp.sum(grad_x * mlp_out, axis=1))
        grad_down_bias = lax.optimization_barrier(jnp.sum(d_mlp, axis=(0, 1)))
        d_mlp_low = d_mlp.astype(jnp.bfloat16).reshape(all_rows, D)
        grad_down = jnp.dot(gelu_low.T, d_mlp_low, preferred_element_type=jnp.float32)
        d_gelu = jnp.dot(d_mlp_low, down_weight[current].T, preferred_element_type=jnp.float32)
        d_pre = d_gelu * gelu_slope(pre_act)
        grad_up_bias = lax.optimization_barrier(jnp.sum(d_pre, axis=0))
        d_pre_low = d_pre.astype(jnp.bfloat16)
        grad_up = jnp.dot(mlp_in.T, d_pre_low, preferred_element_type=jnp.float32)
        d_mlp_in = group_sum([d_pre_low], [up_weight[current]]).reshape(latent_count, SEQ, D)
        d_shift_mlp = lax.optimization_barrier(jnp.sum(d_mlp_in, axis=1))
        d_scale_mlp = lax.optimization_barrier(jnp.sum(d_mlp_in * normed_mlp, axis=1))
        d_middle = grad_x + norm_back(normed_mlp, inverse_mlp, d_mlp_in * (1.0 + scale_mlp))
        d_attn = d_middle * gate_attn
        d_gate_attn = lax.optimization_barrier(jnp.sum(d_middle * attn_out, axis=1))
        grad_proj_bias = lax.optimization_barrier(jnp.sum(d_attn, axis=(0, 1)))
        d_attn_low = d_attn.astype(jnp.bfloat16).reshape(all_rows, D)
        grad_proj = jnp.dot(attended.T, d_attn_low, preferred_element_type=jnp.float32)
        d_attended = jnp.dot(d_attn_low, proj_weight[current].T, preferred_element_type=jnp.float32).astype(jnp.bfloat16)
        query_heads = widen(split_heads(queries, latent_count))
        key_heads = widen(split_heads(key_rows, latent_count))
        value_heads = widen(split_heads(value_rows, latent_count))
        scores = jnp.einsum('bqhd,bkhd->bhqk', query_heads, key_heads) * score_scale
        prob_full = jnp.exp(scores - log_total)
        prob_wide = widen(prob_full.astype(jnp.bfloat16))
        d_heads = widen(split_heads(d_attended, latent_count))
        grad_value = jnp.einsum('bhqk,bqhd->bkhd', prob_wide, d_heads).reshape(all_rows, D)
        d_prob = jnp.einsum('bqhd,bkhd->bhqk', d_heads, value_heads)
        row_delta = jnp.einsum('bqhd,bqhd->bhq', d_heads, widen(split_heads(attended, latent_count)))
        d_scores = prob_full * (d_prob - row_delta[..., None])
        d_score_wide = widen(d_scores.astype(jnp.bfloat16))
        grad_query = jnp.einsum('bhqk,bkhd->bqhd', d_score_wide, key_heads).reshape(all_rows, D) * score_scale
        grad_key = jnp.einsum('bhqk,bqhd->bkhd', d_score_wide, query_heads).reshape(all_rows, D) * score_scale
        grad_qv_bias = jnp.stack([lax.optimization_barrier(jnp.sum(grad_query, axis=0)), lax.optimization_barrier(jnp.sum(grad_value, axis=0))])
        query_low = grad_query.astype(jnp.bfloat16)
        key_low = grad_key.astype(jnp.bfloat16)
        value_low = grad_value.astype(jnp.bfloat16)
        grad_qkv = jnp.stack([jnp.dot(attn_in.T, query_low, preferred_element_type=jnp.float32), jnp.dot(attn_in.T, key_low, preferred_element_type=jnp.float32), jnp.dot(attn_in.T, value_low, preferred_element_type=jnp.float32)])
        d_attn_in = group_sum([query_low, key_low, value_low], [qkv_weight[current, 0], qkv_weight[current, 1], qkv_weight[current, 2]])
        d_attn_in = d_attn_in.reshape(latent_count, SEQ, D)
        d_shift_attn = lax.optimization_barrier(jnp.sum(d_attn_in, axis=1))
        d_scale_attn = lax.optimization_barrier(jnp.sum(d_attn_in * normed_attn, axis=1))
        grad_x = d_middle + norm_back(normed_attn, inverse_attn, d_attn_in * (1.0 + scale_attn))
        mod_grads[current] = jnp.concatenate([d_shift_attn, d_scale_attn, d_gate_attn, d_shift_mlp, d_scale_mlp, d_gate_mlp], axis=1)
        layer_grads[current] = (grad_qkv, grad_qv_bias, grad_proj, grad_proj_bias, grad_up, grad_up_bias, grad_down, grad_down_bias)
    stacked = tuple((jnp.stack([layer_grads[current][member] for current in range(LAYERS)]) for member in range(8)))
    return (current_x, grad_x, jnp.stack(mod_grads), stacked)

def reference(tokens, timesteps, labels, time_weight, class_table, mod_weight, mod_bias, qkv_weight, qv_bias, proj_weight, proj_bias, up_weight, up_bias, down_weight, down_bias, grad_output):
    features = time_features(timesteps, FREQ)
    condition = jnp.dot(features, time_weight, precision=PRECISE) + class_table[labels]
    cond_act = jax.nn.silu(condition).astype(jnp.bfloat16)
    modulation = jnp.stack([jnp.dot(cond_act, mod_weight[current], preferred_element_type=jnp.float32) + mod_bias[current] for current in range(LAYERS)])
    block_latents = LAT_DEV
    blocks = LATENTS // block_latents
    token_blocks = tokens.reshape(blocks, block_latents, SEQ, D)
    grad_blocks = grad_output.reshape(blocks, block_latents, SEQ, D)
    mod_blocks = jnp.transpose(modulation.reshape(LAYERS, blocks, block_latents, 6 * D), (1, 0, 2, 3))
    weights = (qkv_weight, qv_bias, proj_weight, proj_bias, up_weight, up_bias, down_weight, down_bias)
    shapes = [(LAYERS, 3, D, D), (LAYERS, 2, D), (LAYERS, D, D), (LAYERS, D), (LAYERS, D, FF), (LAYERS, FF), (LAYERS, FF, D), (LAYERS, D)]
    initial = tuple((jnp.zeros(shape, jnp.float32) for shape in shapes))
    rounded_members = (0, 2, 4, 6)

    def scan_step(running, block_items):
        inputs, grad_rows, mod_rows = block_items
        block_out, grad_in, d_mod, grads_here = block_pass(inputs, grad_rows, mod_rows, weights)
        added = []
        for member in range(8):
            term = grads_here[member]
            if member in rounded_members:
                term = widen(term.astype(jnp.bfloat16))
            added.append(running[member] + term)
        return (tuple(added), (block_out, grad_in, d_mod))
    totals, (block_outs, grad_ins, d_mods) = lax.scan(scan_step, initial, (token_blocks, grad_blocks, mod_blocks))
    d_mod_all = jnp.transpose(d_mods, (1, 0, 2, 3)).reshape(LAYERS, LATENTS, 6 * D)
    cond_wide = widen(cond_act)
    grad_mod_weight = jnp.stack([jnp.dot(cond_wide.T, d_mod_all[current], precision=PRECISE) for current in range(LAYERS)])
    grad_mod_bias = lax.optimization_barrier(jnp.sum(d_mod_all, axis=1))
    cond_back = jnp.dot(d_mod_all[0], mod_weight[0].astype(jnp.float32).T, precision=PRECISE)
    for current in range(1, LAYERS):
        cond_back = cond_back + jnp.dot(d_mod_all[current], mod_weight[current].astype(jnp.float32).T, precision=PRECISE)
    d_condition = cond_back * silu_slope(condition)
    grad_time_weight = jnp.dot(features.T, d_condition, precision=PRECISE)
    one_hot = (labels[:, None] == jnp.arange(CLASSES, dtype=jnp.int32)[None, :]).astype(jnp.float32)
    grad_class_table = jnp.dot(one_hot.T, d_condition, precision=PRECISE)
    output = block_outs.reshape(TOKENS, D)
    grad_tokens = grad_ins.reshape(TOKENS, D)
    return (output, grad_tokens, grad_time_weight, grad_class_table, grad_mod_weight, grad_mod_bias, totals[0], totals[1], totals[2], totals[3], totals[4], totals[5], totals[6], totals[7])
```

```python
import functools
import math

import jax
import jax.numpy as jnp
from jax import lax
from jax.experimental import pallas as pl
from jax.experimental.pallas import tpu as pltpu
from jax.sharding import PartitionSpec as P

HEAD_DIM = 72
SEQ = 256
LAYERS = 1


EPSILON = 1e-06
PRECISE = lax.Precision.HIGHEST
GELU_COEFF = math.sqrt(2.0 / math.pi)
CUBIC_COEFF = 0.044715


def time_features(timesteps, width):
    half_width = width // 2
    freq_rates = jnp.exp(
        -math.log(10000.0) * jnp.arange(half_width, dtype=jnp.float32) / half_width
    )
    angles = timesteps.astype(jnp.float32)[:, None] * freq_rates[None, :]
    return jnp.concatenate([jnp.cos(angles), jnp.sin(angles)], axis=1)


def layer_norm(values):
    average = jnp.mean(values, axis=-1, keepdims=True)
    centred = values - average
    inverse = lax.rsqrt(jnp.mean(centred * centred, axis=-1, keepdims=True) + EPSILON)
    return (centred * inverse, inverse)


def norm_back(normed, inverse, grad_normed):
    first = jnp.mean(grad_normed, axis=-1, keepdims=True)
    second = jnp.mean(grad_normed * normed, axis=-1, keepdims=True)
    return inverse * (grad_normed - first - normed * second)


def gelu_value(values):
    return (
        0.5
        * values
        * (1.0 + jnp.tanh(GELU_COEFF * (values + CUBIC_COEFF * values * values * values)))
    )


def gelu_slope(values):
    tangent = jnp.tanh(GELU_COEFF * (values + CUBIC_COEFF * values * values * values))
    return 0.5 * (1.0 + tangent) + 0.5 * values * (1.0 - tangent * tangent) * GELU_COEFF * (
        1.0 + 3.0 * CUBIC_COEFF * values * values
    )


def silu_slope(values):
    logistic = jax.nn.sigmoid(values)
    return logistic * (1.0 + values * (1.0 - logistic))


MESH = pl.DeviceIdType.MESH
ON_CHIP = pl.BlockSpec(memory_space=pltpu.VMEM)
IN_PLACE = pl.BlockSpec(memory_space=pl.ANY)
DMA = pltpu.SemaphoreType.DMA


def comm_call(body, out_shape, scratch, number, args, in_specs=None, out_specs=None):
    many = isinstance(out_shape, (list, tuple))
    return pl.pallas_call(
        body,
        out_shape=out_shape,
        in_specs=in_specs or [ON_CHIP] * len(args),
        out_specs=out_specs or ([ON_CHIP] * len(out_shape) if many else ON_CHIP),
        scratch_shapes=scratch,
        compiler_params=pltpu.CompilerParams(
            collective_id=number, has_side_effects=True, vmem_limit_bytes=48 * 1024 * 1024
        ),
    )(*args)


def greet(peers):
    barrier = pltpu.get_barrier_semaphore()
    for peer in peers:
        pl.semaphore_signal(barrier, inc=1, device_id=peer, device_id_type=MESH)
    pl.semaphore_wait(barrier, len(peers))


def push(source, target, send_sem, recv_sem, peer):
    copy = pltpu.make_async_remote_copy(
        src_ref=source,
        dst_ref=target,
        send_sem=send_sem,
        recv_sem=recv_sem,
        device_id=peer,
        device_id_type=MESH,
    )
    copy.start()
    return copy


def tensor_ring(tensor_count):
    group = lax.axis_index("dp")
    place = lax.axis_index("tensor")
    cores = 2 if tensor_count % 2 == 0 else 1
    chips = tensor_count // cores
    chip, core = place // cores, lax.rem(place, cores)
    return group, chip, core, chips, cores


def gather_rows_body(tensor_count, own_ref, out_ref, send_sem, recv_sem, local_sem):
    group, chip, core, chips, cores = tensor_ring(tensor_count)
    place = chip * cores + core
    far = [(group, lax.rem(chip + step, chips) * cores + core) for step in range(1, chips)]
    near = [(group, chip * cores + lax.rem(core + step, cores)) for step in range(1, cores)]
    greet(far + near)
    copies = []
    for index, peer in enumerate(far):
        copies.append(push(own_ref, out_ref.at[place], send_sem.at[index], recv_sem.at[index], peer))
    arrivals = list(copies)
    base = len(far)
    for peer in near:
        copies.append(push(own_ref, out_ref.at[place], send_sem.at[base], recv_sem.at[base], peer))
        base += 1
    keep = pltpu.make_async_copy(own_ref, out_ref.at[place], local_sem)
    keep.start()
    for step in range(1, chips):
        arrivals[step - 1].wait_recv()
        block = lax.rem(chip + chips - step, chips) * cores + core
        for peer in near:
            copies.append(
                push(out_ref.at[block], out_ref.at[block], send_sem.at[base], recv_sem.at[base], peer)
            )
            base += 1
    for copy in copies[len(far) :]:
        copy.wait_recv()
    for copy in copies:
        copy.wait_send()
    keep.wait()


def gather_rows(values, number):
    tensor_count = lax.axis_size("tensor")
    rows, cols = values.shape
    gathered = comm_call(
        functools.partial(gather_rows_body, tensor_count),
        jax.ShapeDtypeStruct((tensor_count, rows, cols), values.dtype),
        [DMA((2 * tensor_count,)), DMA((2 * tensor_count,)), DMA],
        number,
        (values,),
    )
    return gathered.reshape(tensor_count * rows, cols)


def scatter_rows_body(
    tensor_count, terms_ref, out_ref, near_ref, sum_ref, far_ref, send_sem, recv_sem
):
    group, chip, core, chips, cores = tensor_ring(tensor_count)
    far = [(group, lax.rem(chip + step, chips) * cores + core) for step in range(1, chips)]
    near = [lax.rem(core + step, cores) for step in range(1, cores)]
    greet(far + [(group, chip * cores + other) for other in near])
    copies = []
    base = 0
    arrivals = []
    for step in list(range(1, chips)) + [0]:
        column = []
        target_chip = lax.rem(chip + step, chips)
        for slot, other in enumerate(near):
            copy = push(
                terms_ref.at[target_chip * cores + other],
                near_ref.at[step, slot],
                send_sem.at[base],
                recv_sem.at[base],
                (group, chip * cores + other),
            )
            base += 1
            column.append(copy)
            copies.append(copy)
        arrivals.append((step, target_chip, column))
    sent_far = []
    for step, target_chip, column in arrivals:
        total = terms_ref[target_chip * cores + core].astype(jnp.float32)
        for slot, copy in enumerate(column):
            copy.wait_recv()
            total = total + near_ref[step, slot].astype(jnp.float32)
        if step:
            sum_ref[step - 1] = total.astype(jnp.bfloat16)
            copy = push(
                sum_ref.at[step - 1],
                far_ref.at[step - 1],
                send_sem.at[base],
                recv_sem.at[base],
                far[step - 1],
            )
            base += 1
            sent_far.append(copy)
            copies.append(copy)
        else:
            out_ref[...] = total
    for slot, copy in enumerate(sent_far):
        copy.wait_recv()
        out_ref[...] += far_ref[slot].astype(jnp.float32)
    for copy in copies:
        copy.wait_send()


def scatter_rows(values, number):
    tensor_count = lax.axis_size("tensor")
    cols = values.shape[1]
    rows = values.shape[0] // tensor_count
    cores = 2 if tensor_count % 2 == 0 else 1
    chips = tensor_count // cores
    return comm_call(
        functools.partial(scatter_rows_body, tensor_count),
        jax.ShapeDtypeStruct((rows, cols), jnp.float32),
        [
            pltpu.VMEM((chips, max(cores - 1, 1), rows, cols), jnp.bfloat16),
            pltpu.VMEM((max(chips - 1, 1), rows, cols), jnp.bfloat16),
            pltpu.VMEM((max(chips - 1, 1), rows, cols), jnp.bfloat16),
            DMA((2 * tensor_count,)),
            DMA((2 * tensor_count,)),
        ],
        number,
        (values.reshape(tensor_count, rows, cols),),
    )


def axis_peers(group_count, tensor_count):
    group, place = lax.axis_index("dp"), lax.axis_index("tensor")
    others = [(lax.rem(group + step, group_count), place) for step in range(1, group_count)]
    mates = [(group, lax.rem(place + step, tensor_count)) for step in range(1, tensor_count)]
    return group, place, others, mates


def modulation_body(
    group_count, tensor_count, terms_ref, out_ref, landed_ref, send_sem, recv_sem, send_two, recv_two
):
    group, place, others, mates = axis_peers(group_count, tensor_count)
    greet(others + mates)
    copies = []
    for index, peer in enumerate(others):
        copies.append(
            push(
                terms_ref.at[peer[0]],
                landed_ref.at[index],
                send_sem.at[index],
                recv_sem.at[index],
                peer,
            )
        )
    total = terms_ref[group]
    for index, copy in enumerate(copies):
        copy.wait_recv()
        total = total + landed_ref[index]
    out_ref[place] = total
    spread = []
    for index, peer in enumerate(mates):
        spread.append(
            push(out_ref.at[place], out_ref.at[place], send_two.at[index], recv_two.at[index], peer)
        )
    for copy in spread:
        copy.wait_recv()
    for copy in copies + spread:
        copy.wait_send()


def sum_modulation(terms, number):
    group_count, tensor_count = lax.axis_size("dp"), lax.axis_size("tensor")
    _, latents, cols = terms.shape
    return comm_call(
        functools.partial(modulation_body, group_count, tensor_count),
        jax.ShapeDtypeStruct((tensor_count, latents, cols), jnp.float32),
        [
            pltpu.VMEM((max(group_count - 1, 1), latents, cols), jnp.float32),
            DMA((group_count,)),
            DMA((group_count,)),
            DMA((tensor_count,)),
            DMA((tensor_count,)),
        ],
        number,
        (terms,),
    )


def collect_body(
    group_count,
    tensor_count,
    split_ref,
    own_ref,
    split_out,
    own_out,
    landed_ref,
    send_sem,
    recv_sem,
    send_two,
    recv_two,
):
    group, place, others, mates = axis_peers(group_count, tensor_count)
    greet(others + mates)
    copies = []
    for index, peer in enumerate(others):
        copies.append(
            push(own_ref, own_out.at[group], send_two.at[index], recv_two.at[index], peer)
        )
    first = []
    for index, peer in enumerate(mates):
        first.append(
            push(
                split_ref.at[peer[1]],
                landed_ref.at[index],
                send_sem.at[index],
                recv_sem.at[index],
                peer,
            )
        )
    own_out[group] = own_ref[...]
    total = split_ref[place]
    for index, copy in enumerate(first):
        copy.wait_recv()
        total = total + landed_ref[index]
    split_out[group] = total
    count = len(others)
    for index, peer in enumerate(others):
        copies.append(
            push(
                split_out.at[group],
                split_out.at[group],
                send_two.at[count + index],
                recv_two.at[count + index],
                peer,
            )
        )
    for copy in copies:
        copy.wait_recv()
    for copy in copies + first:
        copy.wait_send()


def collect(split, own, number):
    group_count, tensor_count = lax.axis_size("dp"), lax.axis_size("tensor")
    wide, narrow = split.shape[2], own.shape[1]
    return comm_call(
        functools.partial(collect_body, group_count, tensor_count),
        [
            jax.ShapeDtypeStruct((group_count, 1, wide), jnp.float32),
            jax.ShapeDtypeStruct((group_count, 1, narrow), jnp.float32),
        ],
        [
            pltpu.VMEM((max(tensor_count - 1, 1), 1, wide), jnp.float32),
            DMA((tensor_count,)),
            DMA((tensor_count,)),
            DMA((2 * group_count,)),
            DMA((2 * group_count,)),
        ],
        number,
        (split, own),
    )


def spread_body(group_count, tensor_count, one_ref, two_ref, one_out, two_out, send_sem, recv_sem):
    group, place, others, mates = axis_peers(group_count, tensor_count)
    greet(mates)
    copies = []
    count = len(mates)
    for index, peer in enumerate(mates):
        copies.append(
            push(one_ref, one_out.at[place], send_sem.at[index], recv_sem.at[index], peer)
        )
        copies.append(
            push(
                two_ref,
                two_out.at[place],
                send_sem.at[count + index],
                recv_sem.at[count + index],
                peer,
            )
        )
    one_out[place] = one_ref[...]
    two_out[place] = two_ref[...]
    for copy in copies:
        copy.wait_recv()
    for copy in copies:
        copy.wait_send()


def spread_pair(one, two, number):
    group_count, tensor_count = lax.axis_size("dp"), lax.axis_size("tensor")
    return comm_call(
        functools.partial(spread_body, group_count, tensor_count),
        [
            jax.ShapeDtypeStruct((tensor_count,) + one.shape, jnp.float32),
            jax.ShapeDtypeStruct((tensor_count,) + two.shape, jnp.float32),
        ],
        [DMA((2 * tensor_count,)), DMA((2 * tensor_count,))],
        number,
        (one, two),
    )


def gather_weight(weight):
    return lax.all_gather(weight, "dp", axis=0, tiled=True)


def scatter_weight(grad):
    return lax.psum_scatter(
        grad.astype(jnp.bfloat16), "dp", scatter_dimension=0, tiled=True
    ).astype(jnp.float32)


def dot_low(left, right, left_dim, right_dim):
    return lax.dot_general(
        left, right, (((left_dim,), (right_dim,)), ((), ())), preferred_element_type=jnp.float32
    )


def split_heads(values, latent_count):
    return values.reshape(latent_count, SEQ, -1, HEAD_DIM)


def local(
    tokens,
    timesteps,
    labels,
    time_weight,
    class_table,
    mod_weight,
    mod_bias,
    qkv_weight,
    qv_bias,
    proj_weight,
    proj_bias,
    up_weight,
    up_bias,
    down_weight,
    down_bias,
    grad_output,
):
    rows_own, model_width = tokens.shape
    tensor_count = lax.axis_size("tensor")
    group_count = lax.axis_size("dp")
    tensor_place = lax.axis_index("tensor")
    group_rows = rows_own * tensor_count
    latent_count = group_rows // SEQ
    head_cols = qkv_weight.shape[3]
    unit_cols = up_weight.shape[2]
    mod_cols = mod_weight.shape[2]
    own_rows = qkv_weight.shape[2]
    head_start = tensor_place * head_cols
    unit_start = tensor_place * unit_cols
    score_scale = 1.0 / math.sqrt(HEAD_DIM)

    attn_own = jnp.concatenate(
        [qkv_weight[0, 0], qkv_weight[0, 1], qkv_weight[0, 2], proj_weight[0].T], axis=1
    )
    attn_full = gather_weight(attn_own)
    up_full = gather_weight(up_weight[0])
    down_full = gather_weight(down_weight[0].T)
    qkv_full = attn_full[:, : 3 * head_cols]
    proj_full = attn_full[:, 3 * head_cols :]

    features = time_features(timesteps, time_weight.shape[0])
    one_hot = (
        labels[:, None] == jnp.arange(class_table.shape[0], dtype=jnp.int32)[None, :]
    ).astype(jnp.float32)
    condition = jnp.dot(features, time_weight, precision=PRECISE) + jnp.dot(
        one_hot, class_table, precision=PRECISE
    )
    cond_act = jax.nn.silu(condition).astype(jnp.bfloat16)
    mod_terms = jnp.dot(cond_act, mod_weight[0], preferred_element_type=jnp.float32)
    mod_sum = sum_modulation(mod_terms.reshape(group_count, latent_count, mod_cols), 1)
    modulation = mod_sum.transpose(1, 0, 2).reshape(latent_count, -1) + mod_bias

    if SEQ % rows_own == 0:
        my_latent = (tensor_place * rows_own) // SEQ
        rows_mod = lax.dynamic_slice_in_dim(modulation, my_latent, 1, 0)
        mine = (jnp.arange(latent_count, dtype=jnp.int32) == my_latent)[:, None]

        def per_latent(values):
            return jnp.where(mine, jnp.sum(values, axis=0)[None, :], 0.0)

    else:
        row_latent = (tensor_place * rows_own + jnp.arange(rows_own, dtype=jnp.int32)) // SEQ
        selector = (
            row_latent[:, None] == jnp.arange(latent_count, dtype=jnp.int32)[None, :]
        ).astype(jnp.float32)
        rows_mod = jnp.dot(selector, modulation, precision=PRECISE)

        def per_latent(values):
            return jnp.dot(selector.T, values, precision=PRECISE)

    shift_attn, scale_attn, gate_attn, shift_mlp, scale_mlp, gate_mlp = [
        rows_mod[:, segment * model_width : (segment + 1) * model_width] for segment in range(6)
    ]

    def attention_scores(queries, key_rows):
        return (
            jnp.einsum(
                "bqhd,bkhd->bhqk",
                split_heads(queries, latent_count),
                split_heads(key_rows, latent_count),
                preferred_element_type=jnp.float32,
            )
            * score_scale
        )

    bias_query = lax.dynamic_slice_in_dim(qv_bias[0, 0], head_start, head_cols, 0)
    bias_value = lax.dynamic_slice_in_dim(qv_bias[0, 1], head_start, head_cols, 0)
    unit_bias = lax.dynamic_slice_in_dim(up_bias[0], unit_start, unit_cols, 0)
    bias_qkv = jnp.concatenate([bias_query, jnp.zeros_like(bias_query), bias_value])

    normed_attn, inverse_attn = layer_norm(tokens)
    attn_in = gather_rows((normed_attn * (1.0 + scale_attn) + shift_attn).astype(jnp.bfloat16), 2)
    qkv_rows = (dot_low(attn_in, qkv_full, 1, 0) + bias_qkv).astype(jnp.bfloat16)
    queries = qkv_rows[:, :head_cols]
    key_rows = qkv_rows[:, head_cols : 2 * head_cols]
    value_rows = qkv_rows[:, 2 * head_cols :]
    scores = attention_scores(queries, key_rows)
    log_total = jnp.log(jnp.sum(jnp.exp(scores), axis=-1, keepdims=True))
    prob_full = jnp.exp(scores - log_total)
    prob_low = prob_full.astype(jnp.bfloat16)
    attended = (
        jnp.einsum(
            "bhqk,bkhd->bqhd",
            prob_low,
            split_heads(value_rows, latent_count),
            preferred_element_type=jnp.float32,
        )
        .astype(jnp.bfloat16)
        .reshape(group_rows, head_cols)
    )
    attn_out = (
        scatter_rows(dot_low(attended, proj_full, 1, 1).astype(jnp.bfloat16), 3) + proj_bias[0]
    )
    middle = tokens + gate_attn * attn_out
    normed_mlp, inverse_mlp = layer_norm(middle)
    mlp_in = gather_rows((normed_mlp * (1.0 + scale_mlp) + shift_mlp).astype(jnp.bfloat16), 4)
    pre_act = dot_low(mlp_in, up_full, 1, 0) + unit_bias
    gelu_low = gelu_value(pre_act).astype(jnp.bfloat16)
    mlp_out = (
        scatter_rows(dot_low(gelu_low, down_full, 1, 1).astype(jnp.bfloat16), 5) + down_bias[0]
    )
    output = middle + gate_mlp * mlp_out

    d_mlp = grad_output * gate_mlp
    d_gate_mlp = per_latent(grad_output * mlp_out)
    down_bias_part = jnp.sum(d_mlp, axis=0)
    d_mlp_all = gather_rows(d_mlp.astype(jnp.bfloat16), 6)
    grad_down = scatter_weight(dot_low(d_mlp_all, gelu_low, 0, 0))
    d_gelu = dot_low(d_mlp_all, down_full, 1, 0)
    d_pre = d_gelu * gelu_slope(pre_act)
    unit_part = jnp.sum(d_pre, axis=0)
    d_pre_low = d_pre.astype(jnp.bfloat16)
    grad_up = scatter_weight(dot_low(mlp_in, d_pre_low, 0, 0))
    d_mlp_in = scatter_rows(dot_low(d_pre_low, up_full, 1, 1).astype(jnp.bfloat16), 7)
    d_shift_mlp = per_latent(d_mlp_in)
    d_scale_mlp = per_latent(d_mlp_in * normed_mlp)
    d_middle = grad_output + norm_back(normed_mlp, inverse_mlp, d_mlp_in * (1.0 + scale_mlp))
    d_attn = d_middle * gate_attn
    d_gate_attn = per_latent(d_middle * attn_out)
    proj_bias_part = jnp.sum(d_attn, axis=0)
    d_attn_all = gather_rows(d_attn.astype(jnp.bfloat16), 8)
    d_attended = dot_low(d_attn_all, proj_full, 1, 0).astype(jnp.bfloat16)
    d_heads = split_heads(d_attended, latent_count)
    grad_value = jnp.einsum(
        "bhqk,bqhd->bkhd", prob_low, d_heads, preferred_element_type=jnp.float32
    ).reshape(group_rows, head_cols)
    d_prob = jnp.einsum(
        "bqhd,bkhd->bhqk",
        d_heads,
        split_heads(value_rows, latent_count),
        preferred_element_type=jnp.float32,
    )
    row_delta = jnp.einsum(
        "bqhd,bqhd->bhq",
        d_heads,
        split_heads(attended, latent_count),
        preferred_element_type=jnp.float32,
    )
    d_score_low = (prob_full * (d_prob - row_delta[..., None])).astype(jnp.bfloat16)
    grad_query = (
        jnp.einsum(
            "bhqk,bkhd->bqhd",
            d_score_low,
            split_heads(key_rows, latent_count),
            preferred_element_type=jnp.float32,
        ).reshape(group_rows, head_cols)
        * score_scale
    )
    grad_key = (
        jnp.einsum(
            "bhqk,bqhd->bkhd",
            d_score_low,
            split_heads(queries, latent_count),
            preferred_element_type=jnp.float32,
        ).reshape(group_rows, head_cols)
        * score_scale
    )
    qv_part = jnp.concatenate([jnp.sum(grad_query, axis=0), jnp.sum(grad_value, axis=0)])
    low_rows = jnp.concatenate(
        [
            grad_query.astype(jnp.bfloat16),
            grad_key.astype(jnp.bfloat16),
            grad_value.astype(jnp.bfloat16),
        ],
        axis=1,
    )
    grad_attn = scatter_weight(
        jnp.concatenate(
            [dot_low(attn_in, low_rows, 0, 0), dot_low(d_attn_all, attended, 0, 0)], axis=1
        )
    )
    d_attn_in = scatter_rows(dot_low(low_rows, qkv_full, 1, 1).astype(jnp.bfloat16), 9)
    d_shift_attn = per_latent(d_attn_in)
    d_scale_attn = per_latent(d_attn_in * normed_attn)
    grad_tokens = d_middle + norm_back(normed_attn, inverse_attn, d_attn_in * (1.0 + scale_attn))

    d_mod_part = jnp.concatenate(
        [d_shift_attn, d_scale_attn, d_gate_attn, d_shift_mlp, d_scale_mlp, d_gate_mlp], axis=1
    )
    bias_cols = model_width // tensor_count
    split = jnp.concatenate(
        [
            d_mod_part[latent].reshape(tensor_count, 1, mod_cols)
            for latent in range(latent_count)
        ]
        + [
            proj_bias_part.reshape(tensor_count, 1, bias_cols),
            down_bias_part.reshape(tensor_count, 1, bias_cols),
        ],
        axis=2,
    )
    own = jnp.concatenate([unit_part, qv_part])[None, :]
    split_all, own_all = collect(split, own, 10)
    mod_end = latent_count * mod_cols
    d_mod_all = split_all[:, 0, :mod_end].reshape(group_count * latent_count, mod_cols)
    totals = jnp.concatenate(
        [
            jnp.sum(d_mod_all, axis=0),
            jnp.sum(split_all[:, 0, mod_end:], axis=0),
            jnp.sum(own_all[:, 0], axis=0),
        ]
    )[None, :]
    cond_wide = cond_act.astype(jnp.float32)
    grad_mod_weight = jnp.dot(cond_wide.T, d_mod_all, precision=PRECISE)[None]
    cond_back = jnp.dot(d_mod_all, mod_weight[0].astype(jnp.float32).T, precision=PRECISE)
    cond_parts, total_parts = spread_pair(cond_back, totals, 11)
    total_parts = total_parts[:, 0]
    ends = [mod_cols, bias_cols, bias_cols, unit_cols, head_cols, head_cols]
    pieces = []
    start = 0
    for width in ends:
        pieces.append(total_parts[:, start : start + width].reshape(1, -1))
        start += width
    modb_total, proj_total, down_total, unit_total, query_total, value_total = pieces
    d_condition = jnp.sum(cond_parts, axis=0) * silu_slope(condition)
    grad_time_weight = jnp.dot(features.T, d_condition, precision=PRECISE)
    grad_class_table = jnp.dot(one_hot.T, d_condition, precision=PRECISE)
    grad_qkv = grad_attn[:, : 3 * head_cols].reshape(own_rows, 3, head_cols).transpose(1, 0, 2)
    return (
        output,
        grad_tokens,
        grad_time_weight,
        grad_class_table,
        grad_mod_weight,
        modb_total,
        grad_qkv[None],
        jnp.concatenate([query_total, value_total])[None],
        grad_attn[:, 3 * head_cols :].T[None],
        proj_total,
        grad_up[None],
        unit_total,
        grad_down.T[None],
        down_total,
    )


def solution(mesh):
    in_specs = (
        P(("dp", "tensor"), None),
        P(),
        P(),
        P(None, "dp"),
        P(None, "dp"),
        P(None, "dp", "tensor"),
        P(),
        P(None, None, "dp", "tensor"),
        P(),
        P(None, "tensor", "dp"),
        P(),
        P(None, "dp", "tensor"),
        P(),
        P(None, "tensor", "dp"),
        P(),
        P(("dp", "tensor"), None),
    )
    out_specs = (
        P(("dp", "tensor"), None),
        P(("dp", "tensor"), None),
        P(None, "dp"),
        P(None, "dp"),
        P(None, "dp", "tensor"),
        P(),
        P(None, None, "dp", "tensor"),
        P(),
        P(None, "tensor", "dp"),
        P(),
        P(None, "dp", "tensor"),
        P(),
        P(None, "tensor", "dp"),
        P(),
    )
    return jax.shard_map(local, mesh=mesh, in_specs=in_specs, out_specs=out_specs, check_vma=False)
```

```python
import functools
import math

import jax
import jax.numpy as jnp
from jax import lax
from jax.experimental import pallas as pl
from jax.experimental.pallas import tpu as pltpu
from jax.sharding import PartitionSpec as P

HEAD_DIM = 72
SEQ = 256
LAYERS = 1


EPSILON = 1e-06
PRECISE = lax.Precision.HIGHEST
GELU_COEFF = math.sqrt(2.0 / math.pi)
CUBIC_COEFF = 0.044715


def time_features(timesteps, width):
    half_width = width // 2
    freq_rates = jnp.exp(
        -math.log(10000.0) * jnp.arange(half_width, dtype=jnp.float32) / half_width
    )
    angles = timesteps.astype(jnp.float32)[:, None] * freq_rates[None, :]
    return jnp.concatenate([jnp.cos(angles), jnp.sin(angles)], axis=1)


def layer_norm(values):
    average = jnp.mean(values, axis=-1, keepdims=True)
    centred = values - average
    inverse = lax.rsqrt(jnp.mean(centred * centred, axis=-1, keepdims=True) + EPSILON)
    return (centred * inverse, inverse)


def norm_back(normed, inverse, grad_normed):
    first = jnp.mean(grad_normed, axis=-1, keepdims=True)
    second = jnp.mean(grad_normed * normed, axis=-1, keepdims=True)
    return inverse * (grad_normed - first - normed * second)


def gelu_value(values):
    return (
        0.5
        * values
        * (1.0 + jnp.tanh(GELU_COEFF * (values + CUBIC_COEFF * values * values * values)))
    )


def gelu_slope(values):
    tangent = jnp.tanh(GELU_COEFF * (values + CUBIC_COEFF * values * values * values))
    return 0.5 * (1.0 + tangent) + 0.5 * values * (1.0 - tangent * tangent) * GELU_COEFF * (
        1.0 + 3.0 * CUBIC_COEFF * values * values
    )


def silu_slope(values):
    logistic = jax.nn.sigmoid(values)
    return logistic * (1.0 + values * (1.0 - logistic))


MESH = pl.DeviceIdType.MESH
ON_CHIP = pl.BlockSpec(memory_space=pltpu.VMEM)
IN_PLACE = pl.BlockSpec(memory_space=pl.ANY)
DMA = pltpu.SemaphoreType.DMA


def comm_call(body, out_shape, scratch, number, args, in_specs=None, out_specs=None):
    many = isinstance(out_shape, (list, tuple))
    return pl.pallas_call(
        body,
        out_shape=out_shape,
        in_specs=in_specs or [ON_CHIP] * len(args),
        out_specs=out_specs or ([ON_CHIP] * len(out_shape) if many else ON_CHIP),
        scratch_shapes=scratch,
        compiler_params=pltpu.CompilerParams(
            collective_id=number, has_side_effects=True, vmem_limit_bytes=48 * 1024 * 1024
        ),
    )(*args)


def greet(peers):
    barrier = pltpu.get_barrier_semaphore()
    for peer in peers:
        pl.semaphore_signal(barrier, inc=1, device_id=peer, device_id_type=MESH)
    pl.semaphore_wait(barrier, len(peers))


def push(source, target, send_sem, recv_sem, peer):
    copy = pltpu.make_async_remote_copy(
        src_ref=source,
        dst_ref=target,
        send_sem=send_sem,
        recv_sem=recv_sem,
        device_id=peer,
        device_id_type=MESH,
    )
    copy.start()
    return copy


def split_axis(axis, count):
    inner = 2 if axis == "tensor" and count % 2 == 0 else count // math.gcd(count, 4)
    return count // inner, inner


def axis_place(axis, place):
    if axis == "tensor":
        return (lax.axis_index("dp"), place)
    return (place, lax.axis_index("tensor"))


def level_peers(axis, count):
    outer, inner = split_axis(axis, count)
    place = lax.axis_index(axis)
    high, low = place // inner, lax.rem(place, inner)
    far = [axis_place(axis, lax.rem(high + step, outer) * inner + low) for step in range(1, outer)]
    near = [axis_place(axis, high * inner + lax.rem(low + step, inner)) for step in range(1, inner)]
    return place, high, low, far, near


def parts_of(rows, most):
    return most if rows % (most * 16) == 0 else 1


def start_gather(axis, count, parts, own_ref, out_ref, send_sem, recv_sem, local_sem):
    outer, inner = split_axis(axis, count)
    place, high, low, far, near = level_peers(axis, count)
    rows = own_ref.shape[0] // parts
    used = iter(range(parts * count))
    first = []
    others = []
    for part in range(parts):
        span = pl.ds(part * rows, rows)
        for step, peer in enumerate(far):
            index = next(used)
            copy = push(
                own_ref.at[span],
                out_ref.at[place, span],
                send_sem.at[index],
                recv_sem.at[index],
                peer,
            )
            first.append((step + 1, span, copy))
        for peer in near:
            index = next(used)
            others.append(
                push(
                    own_ref.at[span],
                    out_ref.at[place, span],
                    send_sem.at[index],
                    recv_sem.at[index],
                    peer,
                )
            )
    keep = pltpu.make_async_copy(own_ref, out_ref.at[place], local_sem)
    keep.start()

    def finish():
        for step, span, copy in first:
            copy.wait_recv()
            block = lax.rem(high + outer - step, outer) * inner + low
            for peer in near:
                index = next(used)
                others.append(
                    push(
                        out_ref.at[block, span],
                        out_ref.at[block, span],
                        send_sem.at[index],
                        recv_sem.at[index],
                        peer,
                    )
                )
        for copy in others:
            copy.wait_recv()
        for copy in others + [copy for _, _, copy in first]:
            copy.wait_send()
        keep.wait()

    return finish


def gather_rows_body(axis, count, parts, own_ref, out_ref, send_sem, recv_sem, local_sem):
    _, _, _, far, near = level_peers(axis, count)
    greet(far + near)
    start_gather(axis, count, parts, own_ref, out_ref, send_sem, recv_sem, local_sem)()


def gather_rows(values, number):
    tensor_count = lax.axis_size("tensor")
    rows, cols = values.shape
    parts = parts_of(rows, 2)
    gathered = comm_call(
        functools.partial(gather_rows_body, "tensor", tensor_count, parts),
        jax.ShapeDtypeStruct((tensor_count, rows, cols), values.dtype),
        [DMA((parts * tensor_count,)), DMA((parts * tensor_count,)), DMA],
        number,
        (values,),
    )
    return gathered.reshape(tensor_count * rows, cols)


def scatter_rows_body(
    axis, count, parts, terms_ref, out_ref, near_ref, sum_ref, far_ref, send_sem, recv_sem
):
    outer, inner = split_axis(axis, count)
    place, high, low, far, near = level_peers(axis, count)
    rows = terms_ref.shape[1] // parts
    greet(far + near)
    used = iter(range(parts * 2 * count))
    copies = []
    arrivals = []
    for part in range(parts):
        span = pl.ds(part * rows, rows)
        for step in list(range(1, outer)) + [0]:
            target = lax.rem(high + step, outer) * inner
            column = []
            for slot, peer in enumerate(near):
                index = next(used)
                other = lax.rem(low + slot + 1, inner)
                column.append(
                    push(
                        terms_ref.at[target + other, span],
                        near_ref.at[step, slot, span],
                        send_sem.at[index],
                        recv_sem.at[index],
                        peer,
                    )
                )
            copies += column
            arrivals.append((step, span, target + low, column))
    sent_far = []
    for step, span, block, column in arrivals:
        total = terms_ref[block, span].astype(jnp.float32)
        for slot, copy in enumerate(column):
            copy.wait_recv()
            total = total + near_ref[step, slot, span].astype(jnp.float32)
        if step:
            sum_ref[step - 1, span] = total.astype(jnp.bfloat16)
            index = next(used)
            copy = push(
                sum_ref.at[step - 1, span],
                far_ref.at[step - 1, span],
                send_sem.at[index],
                recv_sem.at[index],
                far[step - 1],
            )
            sent_far.append((step - 1, span, copy))
            copies.append(copy)
        else:
            out_ref[span] = total
    for slot, span, copy in sent_far:
        copy.wait_recv()
        out_ref[span] += far_ref[slot, span].astype(jnp.float32)
    for copy in copies:
        copy.wait_send()


def scatter_rows(values, number, axis="tensor", most=2):
    count = lax.axis_size(axis)
    cols = values.shape[1]
    rows = values.shape[0] // count
    outer, inner = split_axis(axis, count)
    parts = parts_of(rows, most)
    return comm_call(
        functools.partial(scatter_rows_body, axis, count, parts),
        jax.ShapeDtypeStruct((rows, cols), jnp.float32),
        [
            pltpu.VMEM((outer, max(inner - 1, 1), rows, cols), jnp.bfloat16),
            pltpu.VMEM((max(outer - 1, 1), rows, cols), jnp.bfloat16),
            pltpu.VMEM((max(outer - 1, 1), rows, cols), jnp.bfloat16),
            DMA((parts * 2 * count,)),
            DMA((parts * 2 * count,)),
        ],
        number,
        (values.reshape(count, rows, cols),),
    )


def axis_peers(group_count, tensor_count):
    group, place = lax.axis_index("dp"), lax.axis_index("tensor")
    others = [(lax.rem(group + step, group_count), place) for step in range(1, group_count)]
    mates = [(group, lax.rem(place + step, tensor_count)) for step in range(1, tensor_count)]
    return group, place, others, mates


def modulation_body(
    group_count,
    tensor_count,
    parts,
    terms_ref,
    weight_ref,
    out_ref,
    full_ref,
    landed_ref,
    send_sem,
    recv_sem,
    send_two,
    recv_two,
    send_bulk,
    recv_bulk,
    local_sem,
):
    group, place, others, mates = axis_peers(group_count, tensor_count)
    greet(others + mates)
    copies = []
    for index, peer in enumerate(others):
        copies.append(
            push(
                terms_ref.at[peer[0]],
                landed_ref.at[index],
                send_sem.at[index],
                recv_sem.at[index],
                peer,
            )
        )
    finish = start_gather(
        "dp", group_count, parts, weight_ref, full_ref, send_bulk, recv_bulk, local_sem
    )
    total = terms_ref[group]
    for index, copy in enumerate(copies):
        copy.wait_recv()
        total = total + landed_ref[index]
    out_ref[place] = total
    spread = []
    for index, peer in enumerate(mates):
        spread.append(
            push(out_ref.at[place], out_ref.at[place], send_two.at[index], recv_two.at[index], peer)
        )
    finish()
    for copy in spread:
        copy.wait_recv()
    for copy in copies + spread:
        copy.wait_send()


def sum_modulation(terms, weight, number):
    group_count, tensor_count = lax.axis_size("dp"), lax.axis_size("tensor")
    _, latents, cols = terms.shape
    rows, width = weight.shape
    parts = parts_of(rows, 3)
    summed, full = comm_call(
        functools.partial(modulation_body, group_count, tensor_count, parts),
        [
            jax.ShapeDtypeStruct((tensor_count, latents, cols), jnp.float32),
            jax.ShapeDtypeStruct((group_count, rows, width), weight.dtype),
        ],
        [
            pltpu.VMEM((max(group_count - 1, 1), latents, cols), jnp.float32),
            DMA((group_count,)),
            DMA((group_count,)),
            DMA((tensor_count,)),
            DMA((tensor_count,)),
            DMA((parts * group_count,)),
            DMA((parts * group_count,)),
            DMA,
        ],
        number,
        (terms, weight),
    )
    return summed, full.reshape(group_count * rows, width)


def collect_body(
    group_count,
    tensor_count,
    split_ref,
    own_ref,
    split_out,
    own_out,
    landed_ref,
    send_sem,
    recv_sem,
    send_two,
    recv_two,
):
    group, place, others, mates = axis_peers(group_count, tensor_count)
    greet(others + mates)
    copies = []
    for index, peer in enumerate(others):
        copies.append(
            push(own_ref, own_out.at[group], send_two.at[index], recv_two.at[index], peer)
        )
    first = []
    for index, peer in enumerate(mates):
        first.append(
            push(
                split_ref.at[peer[1]],
                landed_ref.at[index],
                send_sem.at[index],
                recv_sem.at[index],
                peer,
            )
        )
    own_out[group] = own_ref[...]
    total = split_ref[place]
    for index, copy in enumerate(first):
        copy.wait_recv()
        total = total + landed_ref[index]
    split_out[group] = total
    count = len(others)
    for index, peer in enumerate(others):
        copies.append(
            push(
                split_out.at[group],
                split_out.at[group],
                send_two.at[count + index],
                recv_two.at[count + index],
                peer,
            )
        )
    for copy in copies:
        copy.wait_recv()
    for copy in copies + first:
        copy.wait_send()


def collect(split, own, number):
    group_count, tensor_count = lax.axis_size("dp"), lax.axis_size("tensor")
    wide, narrow = split.shape[2], own.shape[1]
    return comm_call(
        functools.partial(collect_body, group_count, tensor_count),
        [
            jax.ShapeDtypeStruct((group_count, 1, wide), jnp.float32),
            jax.ShapeDtypeStruct((group_count, 1, narrow), jnp.float32),
        ],
        [
            pltpu.VMEM((max(tensor_count - 1, 1), 1, wide), jnp.float32),
            DMA((tensor_count,)),
            DMA((tensor_count,)),
            DMA((2 * group_count,)),
            DMA((2 * group_count,)),
        ],
        number,
        (split, own),
    )


def spread_body(group_count, tensor_count, one_ref, two_ref, one_out, two_out, send_sem, recv_sem):
    group, place, others, mates = axis_peers(group_count, tensor_count)
    greet(mates)
    copies = []
    count = len(mates)
    for index, peer in enumerate(mates):
        copies.append(
            push(one_ref, one_out.at[place], send_sem.at[index], recv_sem.at[index], peer)
        )
        copies.append(
            push(
                two_ref,
                two_out.at[place],
                send_sem.at[count + index],
                recv_sem.at[count + index],
                peer,
            )
        )
    one_out[place] = one_ref[...]
    two_out[place] = two_ref[...]
    for copy in copies:
        copy.wait_recv()
    for copy in copies:
        copy.wait_send()


def spread_pair(one, two, number):
    group_count, tensor_count = lax.axis_size("dp"), lax.axis_size("tensor")
    return comm_call(
        functools.partial(spread_body, group_count, tensor_count),
        [
            jax.ShapeDtypeStruct((tensor_count,) + one.shape, jnp.float32),
            jax.ShapeDtypeStruct((tensor_count,) + two.shape, jnp.float32),
        ],
        [DMA((2 * tensor_count,)), DMA((2 * tensor_count,))],
        number,
        (one, two),
    )


def gather_weight(weight):
    return lax.all_gather(weight, "dp", axis=0, tiled=True)


def scatter_weight(grad):
    return lax.psum_scatter(grad, "dp", scatter_dimension=0, tiled=True).astype(jnp.float32)


def dot_low(left, right, left_dim, right_dim):
    return lax.dot_general(
        left, right, (((left_dim,), (right_dim,)), ((), ())), preferred_element_type=jnp.float32
    )


def split_heads(values, latent_count):
    return values.reshape(latent_count, SEQ, -1, HEAD_DIM)


def local(
    tokens,
    timesteps,
    labels,
    time_weight,
    class_table,
    mod_weight,
    mod_bias,
    qkv_weight,
    qv_bias,
    proj_weight,
    proj_bias,
    up_weight,
    up_bias,
    down_weight,
    down_bias,
    grad_output,
):
    rows_own, model_width = tokens.shape
    tensor_count = lax.axis_size("tensor")
    group_count = lax.axis_size("dp")
    tensor_place = lax.axis_index("tensor")
    group_rows = rows_own * tensor_count
    latent_count = group_rows // SEQ
    head_cols = qkv_weight.shape[3]
    unit_cols = up_weight.shape[2]
    mod_cols = mod_weight.shape[2]
    own_rows = qkv_weight.shape[2]
    head_start = tensor_place * head_cols
    unit_start = tensor_place * unit_cols
    score_scale = 1.0 / math.sqrt(HEAD_DIM)

    attn_own = jnp.concatenate(
        [qkv_weight[0, 0], qkv_weight[0, 1], qkv_weight[0, 2], proj_weight[0].T], axis=1
    )
    up_full = gather_weight(up_weight[0])
    down_full = gather_weight(down_weight[0].T)

    features = time_features(timesteps, time_weight.shape[0])
    one_hot = (
        labels[:, None] == jnp.arange(class_table.shape[0], dtype=jnp.int32)[None, :]
    ).astype(jnp.float32)
    condition = jnp.dot(features, time_weight, precision=PRECISE) + jnp.dot(
        one_hot, class_table, precision=PRECISE
    )
    cond_act = jax.nn.silu(condition).astype(jnp.bfloat16)
    mod_terms = jnp.dot(cond_act, mod_weight[0], preferred_element_type=jnp.float32)
    mod_sum, attn_full = sum_modulation(
        mod_terms.reshape(group_count, latent_count, mod_cols), attn_own, 1
    )
    qkv_full = attn_full[:, : 3 * head_cols]
    proj_full = attn_full[:, 3 * head_cols :]
    modulation = mod_sum.transpose(1, 0, 2).reshape(latent_count, -1) + mod_bias

    if SEQ % rows_own == 0:
        my_latent = (tensor_place * rows_own) // SEQ
        rows_mod = lax.dynamic_slice_in_dim(modulation, my_latent, 1, 0)
        mine = (jnp.arange(latent_count, dtype=jnp.int32) == my_latent)[:, None]

        def per_latent(values):
            return jnp.where(mine, jnp.sum(values, axis=0)[None, :], 0.0)

    else:
        row_latent = (tensor_place * rows_own + jnp.arange(rows_own, dtype=jnp.int32)) // SEQ
        selector = (
            row_latent[:, None] == jnp.arange(latent_count, dtype=jnp.int32)[None, :]
        ).astype(jnp.float32)
        rows_mod = jnp.dot(selector, modulation, precision=PRECISE)

        def per_latent(values):
            return jnp.dot(selector.T, values, precision=PRECISE)

    shift_attn, scale_attn, gate_attn, shift_mlp, scale_mlp, gate_mlp = [
        rows_mod[:, segment * model_width : (segment + 1) * model_width] for segment in range(6)
    ]

    def attention_scores(queries, key_rows):
        return (
            jnp.einsum(
                "bqhd,bkhd->bhqk",
                split_heads(queries, latent_count),
                split_heads(key_rows, latent_count),
                preferred_element_type=jnp.float32,
            )
            * score_scale
        )

    bias_query = lax.dynamic_slice_in_dim(qv_bias[0, 0], head_start, head_cols, 0)
    bias_value = lax.dynamic_slice_in_dim(qv_bias[0, 1], head_start, head_cols, 0)
    unit_bias = lax.dynamic_slice_in_dim(up_bias[0], unit_start, unit_cols, 0)
    bias_qkv = jnp.concatenate([bias_query, jnp.zeros_like(bias_query), bias_value])

    normed_attn, inverse_attn = layer_norm(tokens)
    attn_in = gather_rows((normed_attn * (1.0 + scale_attn) + shift_attn).astype(jnp.bfloat16), 2)
    qkv_rows = (dot_low(attn_in, qkv_full, 1, 0) + bias_qkv).astype(jnp.bfloat16)
    queries = qkv_rows[:, :head_cols]
    key_rows = qkv_rows[:, head_cols : 2 * head_cols]
    value_rows = qkv_rows[:, 2 * head_cols :]
    scores = attention_scores(queries, key_rows)
    log_total = jnp.log(jnp.sum(jnp.exp(scores), axis=-1, keepdims=True))
    prob_full = jnp.exp(scores - log_total)
    prob_low = prob_full.astype(jnp.bfloat16)
    attended = (
        jnp.einsum(
            "bhqk,bkhd->bqhd",
            prob_low,
            split_heads(value_rows, latent_count),
            preferred_element_type=jnp.float32,
        )
        .astype(jnp.bfloat16)
        .reshape(group_rows, head_cols)
    )
    attn_out = (
        scatter_rows(dot_low(attended, proj_full, 1, 1).astype(jnp.bfloat16), 3) + proj_bias[0]
    )
    middle = tokens + gate_attn * attn_out
    normed_mlp, inverse_mlp = layer_norm(middle)
    mlp_in = gather_rows((normed_mlp * (1.0 + scale_mlp) + shift_mlp).astype(jnp.bfloat16), 4)
    pre_act = dot_low(mlp_in, up_full, 1, 0) + unit_bias
    gelu_low = gelu_value(pre_act).astype(jnp.bfloat16)
    d_mlp = grad_output * gate_mlp
    down_bias_part = jnp.sum(d_mlp, axis=0)
    d_mlp_all = gather_rows(d_mlp.astype(jnp.bfloat16), 6)
    grad_down_low = dot_low(d_mlp_all, gelu_low, 0, 0).astype(jnp.bfloat16)
    grad_down_low, gelu_low = lax.optimization_barrier((grad_down_low, gelu_low))
    grad_down = scatter_weight(grad_down_low)
    mlp_out = (
        scatter_rows(dot_low(gelu_low, down_full, 1, 1).astype(jnp.bfloat16), 5) + down_bias[0]
    )
    output = middle + gate_mlp * mlp_out

    d_gate_mlp = per_latent(grad_output * mlp_out)
    d_gelu = dot_low(d_mlp_all, down_full, 1, 0)
    d_pre = d_gelu * gelu_slope(pre_act)
    unit_part = jnp.sum(d_pre, axis=0)
    d_pre_low = d_pre.astype(jnp.bfloat16)
    grad_up_low = dot_low(mlp_in, d_pre_low, 0, 0).astype(jnp.bfloat16)
    grad_up_low, d_pre_low = lax.optimization_barrier((grad_up_low, d_pre_low))
    grad_up = scatter_weight(grad_up_low)
    d_mlp_in = scatter_rows(dot_low(d_pre_low, up_full, 1, 1).astype(jnp.bfloat16), 7)
    d_shift_mlp = per_latent(d_mlp_in)
    d_scale_mlp = per_latent(d_mlp_in * normed_mlp)
    d_middle = grad_output + norm_back(normed_mlp, inverse_mlp, d_mlp_in * (1.0 + scale_mlp))
    d_attn = d_middle * gate_attn
    d_gate_attn = per_latent(d_middle * attn_out)
    proj_bias_part = jnp.sum(d_attn, axis=0)
    d_attn_all = gather_rows(d_attn.astype(jnp.bfloat16), 8)
    d_attended = dot_low(d_attn_all, proj_full, 1, 0).astype(jnp.bfloat16)
    d_heads = split_heads(d_attended, latent_count)
    grad_value = jnp.einsum(
        "bhqk,bqhd->bkhd", prob_low, d_heads, preferred_element_type=jnp.float32
    ).reshape(group_rows, head_cols)
    d_prob = jnp.einsum(
        "bqhd,bkhd->bhqk",
        d_heads,
        split_heads(value_rows, latent_count),
        preferred_element_type=jnp.float32,
    )
    row_delta = jnp.einsum(
        "bqhd,bqhd->bhq",
        d_heads,
        split_heads(attended, latent_count),
        preferred_element_type=jnp.float32,
    )
    d_score_low = (prob_full * (d_prob - row_delta[..., None])).astype(jnp.bfloat16)
    grad_query = (
        jnp.einsum(
            "bhqk,bkhd->bqhd",
            d_score_low,
            split_heads(key_rows, latent_count),
            preferred_element_type=jnp.float32,
        ).reshape(group_rows, head_cols)
        * score_scale
    )
    grad_key = (
        jnp.einsum(
            "bhqk,bqhd->bkhd",
            d_score_low,
            split_heads(queries, latent_count),
            preferred_element_type=jnp.float32,
        ).reshape(group_rows, head_cols)
        * score_scale
    )
    qv_part = jnp.concatenate([jnp.sum(grad_query, axis=0), jnp.sum(grad_value, axis=0)])
    low_rows = jnp.concatenate(
        [
            grad_query.astype(jnp.bfloat16),
            grad_key.astype(jnp.bfloat16),
            grad_value.astype(jnp.bfloat16),
        ],
        axis=1,
    )
    grad_attn = scatter_rows(
        jnp.concatenate(
            [
                dot_low(attn_in, low_rows, 0, 0).astype(jnp.bfloat16),
                dot_low(d_attn_all, attended, 0, 0).astype(jnp.bfloat16),
            ],
            axis=1,
        ),
        12,
        "dp",
        3,
    )
    d_attn_in = scatter_rows(dot_low(low_rows, qkv_full, 1, 1).astype(jnp.bfloat16), 9)
    d_shift_attn = per_latent(d_attn_in)
    d_scale_attn = per_latent(d_attn_in * normed_attn)
    grad_tokens = d_middle + norm_back(normed_attn, inverse_attn, d_attn_in * (1.0 + scale_attn))

    d_mod_part = jnp.concatenate(
        [d_shift_attn, d_scale_attn, d_gate_attn, d_shift_mlp, d_scale_mlp, d_gate_mlp], axis=1
    )
    bias_cols = model_width // tensor_count
    split = jnp.concatenate(
        [
            d_mod_part[latent].reshape(tensor_count, 1, mod_cols)
            for latent in range(latent_count)
        ]
        + [
            proj_bias_part.reshape(tensor_count, 1, bias_cols),
            down_bias_part.reshape(tensor_count, 1, bias_cols),
        ],
        axis=2,
    )
    own = jnp.concatenate([unit_part, qv_part])[None, :]
    split_all, own_all = collect(split, own, 10)
    mod_end = latent_count * mod_cols
    d_mod_all = split_all[:, 0, :mod_end].reshape(group_count * latent_count, mod_cols)
    totals = jnp.concatenate(
        [
            jnp.sum(d_mod_all, axis=0),
            jnp.sum(split_all[:, 0, mod_end:], axis=0),
            jnp.sum(own_all[:, 0], axis=0),
        ]
    )[None, :]
    cond_wide = cond_act.astype(jnp.float32)
    grad_mod_weight = jnp.dot(cond_wide.T, d_mod_all, precision=PRECISE)[None]
    cond_back = jnp.dot(d_mod_all, mod_weight[0].astype(jnp.float32).T, precision=PRECISE)
    cond_parts, total_parts = spread_pair(cond_back, totals, 11)
    total_parts = total_parts[:, 0]
    ends = [mod_cols, bias_cols, bias_cols, unit_cols, head_cols, head_cols]
    pieces = []
    start = 0
    for width in ends:
        pieces.append(total_parts[:, start : start + width].reshape(1, -1))
        start += width
    modb_total, proj_total, down_total, unit_total, query_total, value_total = pieces
    d_condition = jnp.sum(cond_parts, axis=0) * silu_slope(condition)
    grad_time_weight = jnp.dot(features.T, d_condition, precision=PRECISE)
    grad_class_table = jnp.dot(one_hot.T, d_condition, precision=PRECISE)
    grad_qkv = grad_attn[:, : 3 * head_cols].reshape(own_rows, 3, head_cols).transpose(1, 0, 2)
    return (
        output,
        grad_tokens,
        grad_time_weight,
        grad_class_table,
        grad_mod_weight,
        modb_total,
        grad_qkv[None],
        jnp.concatenate([query_total, value_total])[None],
        grad_attn[:, 3 * head_cols :].T[None],
        proj_total,
        grad_up[None],
        unit_total,
        grad_down.T[None],
        down_total,
    )


def solution(mesh):
    in_specs = (
        P(("dp", "tensor"), None),
        P(),
        P(),
        P(None, "dp"),
        P(None, "dp"),
        P(None, "dp", "tensor"),
        P(),
        P(None, None, "dp", "tensor"),
        P(),
        P(None, "tensor", "dp"),
        P(),
        P(None, "dp", "tensor"),
        P(),
        P(None, "tensor", "dp"),
        P(),
        P(("dp", "tensor"), None),
    )
    out_specs = (
        P(("dp", "tensor"), None),
        P(("dp", "tensor"), None),
        P(None, "dp"),
        P(None, "dp"),
        P(None, "dp", "tensor"),
        P(),
        P(None, None, "dp", "tensor"),
        P(),
        P(None, "tensor", "dp"),
        P(),
        P(None, "dp", "tensor"),
        P(),
        P(None, "tensor", "dp"),
        P(),
    )
    return jax.shard_map(local, mesh=mesh, in_specs=in_specs, out_specs=out_specs, check_vma=False)
```

```python
import functools
import math

import jax
import jax.numpy as jnp
from jax import lax
from jax.experimental import pallas as pl
from jax.experimental.pallas import tpu as pltpu
from jax.sharding import PartitionSpec as P

HEAD_DIM = 72
SEQ = 256
LAYERS = 1


EPSILON = 1e-06
PRECISE = lax.Precision.HIGHEST
GELU_COEFF = math.sqrt(2.0 / math.pi)
CUBIC_COEFF = 0.044715


def time_features(timesteps, width):
    half_width = width // 2
    freq_rates = jnp.exp(
        -math.log(10000.0) * jnp.arange(half_width, dtype=jnp.float32) / half_width
    )
    angles = timesteps.astype(jnp.float32)[:, None] * freq_rates[None, :]
    return jnp.concatenate([jnp.cos(angles), jnp.sin(angles)], axis=1)


def layer_norm(values):
    average = jnp.mean(values, axis=-1, keepdims=True)
    centred = values - average
    inverse = lax.rsqrt(jnp.mean(centred * centred, axis=-1, keepdims=True) + EPSILON)
    return (centred * inverse, inverse)


def norm_back(normed, inverse, grad_normed):
    first = jnp.mean(grad_normed, axis=-1, keepdims=True)
    second = jnp.mean(grad_normed * normed, axis=-1, keepdims=True)
    return inverse * (grad_normed - first - normed * second)


def gelu_value(values):
    return (
        0.5
        * values
        * (1.0 + jnp.tanh(GELU_COEFF * (values + CUBIC_COEFF * values * values * values)))
    )


def gelu_slope(values):
    tangent = jnp.tanh(GELU_COEFF * (values + CUBIC_COEFF * values * values * values))
    return 0.5 * (1.0 + tangent) + 0.5 * values * (1.0 - tangent * tangent) * GELU_COEFF * (
        1.0 + 3.0 * CUBIC_COEFF * values * values
    )


def silu_slope(values):
    logistic = jax.nn.sigmoid(values)
    return logistic * (1.0 + values * (1.0 - logistic))


MESH = pl.DeviceIdType.MESH
ON_CHIP = pl.BlockSpec(memory_space=pltpu.VMEM)
IN_PLACE = pl.BlockSpec(memory_space=pl.ANY)
DMA = pltpu.SemaphoreType.DMA


def comm_call(body, out_shape, scratch, number, args, in_specs=None, out_specs=None):
    many = isinstance(out_shape, (list, tuple))
    return pl.pallas_call(
        body,
        out_shape=out_shape,
        in_specs=in_specs or [ON_CHIP] * len(args),
        out_specs=out_specs or ([ON_CHIP] * len(out_shape) if many else ON_CHIP),
        scratch_shapes=scratch,
        compiler_params=pltpu.CompilerParams(
            collective_id=number, has_side_effects=True, vmem_limit_bytes=48 * 1024 * 1024
        ),
    )(*args)


def greet(peers):
    barrier = pltpu.get_barrier_semaphore()
    for peer in peers:
        pl.semaphore_signal(barrier, inc=1, device_id=peer, device_id_type=MESH)
    pl.semaphore_wait(barrier, len(peers))


def push(source, target, send_sem, recv_sem, peer):
    copy = pltpu.make_async_remote_copy(
        src_ref=source,
        dst_ref=target,
        send_sem=send_sem,
        recv_sem=recv_sem,
        device_id=peer,
        device_id_type=MESH,
    )
    copy.start()
    return copy


def split_axis(axis, count):
    inner = 2 if axis == "tensor" and count % 2 == 0 else count // math.gcd(count, 4)
    return count // inner, inner


def axis_place(axis, place):
    if axis == "tensor":
        return (lax.axis_index("dp"), place)
    return (place, lax.axis_index("tensor"))


def level_peers(axis, count):
    outer, inner = split_axis(axis, count)
    place = lax.axis_index(axis)
    high, low = place // inner, lax.rem(place, inner)
    far = [axis_place(axis, lax.rem(high + step, outer) * inner + low) for step in range(1, outer)]
    near = [axis_place(axis, high * inner + lax.rem(low + step, inner)) for step in range(1, inner)]
    return place, high, low, far, near


def parts_of(rows, most):
    return most if rows % (most * 16) == 0 else 1


def start_gather(axis, count, parts, own_ref, out_ref, send_sem, recv_sem, local_sem):
    outer, inner = split_axis(axis, count)
    place, high, low, far, near = level_peers(axis, count)
    rows = own_ref.shape[0] // parts
    used = iter(range(parts * count))
    first = []
    others = []
    for part in range(parts):
        span = pl.ds(part * rows, rows)
        for step, peer in enumerate(far):
            index = next(used)
            copy = push(
                own_ref.at[span],
                out_ref.at[place, span],
                send_sem.at[index],
                recv_sem.at[index],
                peer,
            )
            first.append((step + 1, span, copy))
        for peer in near:
            index = next(used)
            others.append(
                push(
                    own_ref.at[span],
                    out_ref.at[place, span],
                    send_sem.at[index],
                    recv_sem.at[index],
                    peer,
                )
            )
    keep = pltpu.make_async_copy(own_ref, out_ref.at[place], local_sem)
    keep.start()

    def finish():
        for step, span, copy in first:
            copy.wait_recv()
            block = lax.rem(high + outer - step, outer) * inner + low
            for peer in near:
                index = next(used)
                others.append(
                    push(
                        out_ref.at[block, span],
                        out_ref.at[block, span],
                        send_sem.at[index],
                        recv_sem.at[index],
                        peer,
                    )
                )
        for copy in others:
            copy.wait_recv()
        for copy in others + [copy for _, _, copy in first]:
            copy.wait_send()
        keep.wait()

    return finish


def gather_rows_body(axis, count, parts, own_ref, out_ref, send_sem, recv_sem, local_sem):
    _, _, _, far, near = level_peers(axis, count)
    greet(far + near)
    start_gather(axis, count, parts, own_ref, out_ref, send_sem, recv_sem, local_sem)()


def gather_rows(values, number):
    tensor_count = lax.axis_size("tensor")
    rows, cols = values.shape
    parts = parts_of(rows, 2)
    gathered = comm_call(
        functools.partial(gather_rows_body, "tensor", tensor_count, parts),
        jax.ShapeDtypeStruct((tensor_count, rows, cols), values.dtype),
        [DMA((parts * tensor_count,)), DMA((parts * tensor_count,)), DMA],
        number,
        (values,),
    )
    return gathered.reshape(tensor_count * rows, cols)


def gather_both_body(
    counts,
    parts,
    rows_ref,
    weight_ref,
    rows_out,
    weight_out,
    send_sem,
    recv_sem,
    local_sem,
    send_two,
    recv_two,
    local_two,
):
    peers = []
    for axis, count in zip(("tensor", "dp"), counts):
        _, _, _, far, near = level_peers(axis, count)
        peers += far + near
    greet(peers)
    first = start_gather(
        "tensor", counts[0], parts[0], rows_ref, rows_out, send_sem, recv_sem, local_sem
    )
    second = start_gather(
        "dp", counts[1], parts[1], weight_ref, weight_out, send_two, recv_two, local_two
    )
    first()
    second()


def gather_both(values, weight, number):
    counts = (lax.axis_size("tensor"), lax.axis_size("dp"))
    shapes = (values.shape, weight.shape)
    parts = (parts_of(shapes[0][0], 2), parts_of(shapes[1][0], 3))
    scratch = []
    for count, part in zip(counts, parts):
        scratch += [DMA((part * count,)), DMA((part * count,)), DMA]
    one, two = comm_call(
        functools.partial(gather_both_body, counts, parts),
        [
            jax.ShapeDtypeStruct((counts[0],) + shapes[0], values.dtype),
            jax.ShapeDtypeStruct((counts[1],) + shapes[1], weight.dtype),
        ],
        scratch,
        number,
        (values, weight),
    )
    return one.reshape(-1, shapes[0][1]), two.reshape(-1, shapes[1][1])


def start_scatter(
    axis, count, parts, terms_ref, out_ref, near_ref, sum_ref, far_ref, send_sem, recv_sem
):
    outer, inner = split_axis(axis, count)
    place, high, low, far, near = level_peers(axis, count)
    rows = terms_ref.shape[1] // parts
    used = iter(range(parts * 2 * count))
    copies = []
    arrivals = []
    for part in range(parts):
        span = pl.ds(part * rows, rows)
        for step in list(range(1, outer)) + [0]:
            target = lax.rem(high + step, outer) * inner
            column = []
            for slot, peer in enumerate(near):
                index = next(used)
                other = lax.rem(low + slot + 1, inner)
                column.append(
                    push(
                        terms_ref.at[target + other, span],
                        near_ref.at[step, slot, span],
                        send_sem.at[index],
                        recv_sem.at[index],
                        peer,
                    )
                )
            copies += column
            arrivals.append((step, span, target + low, column))

    def finish():
        sent_far = []
        for step, span, block, column in arrivals:
            total = terms_ref[block, span].astype(jnp.float32)
            for slot, copy in enumerate(column):
                copy.wait_recv()
                total = total + near_ref[step, slot, span].astype(jnp.float32)
            if step:
                sum_ref[step - 1, span] = total.astype(jnp.bfloat16)
                index = next(used)
                copy = push(
                    sum_ref.at[step - 1, span],
                    far_ref.at[step - 1, span],
                    send_sem.at[index],
                    recv_sem.at[index],
                    far[step - 1],
                )
                sent_far.append((step - 1, span, copy))
                copies.append(copy)
            else:
                out_ref[span] = total
        for slot, span, copy in sent_far:
            copy.wait_recv()
            out_ref[span] += far_ref[slot, span].astype(jnp.float32)
        for copy in copies:
            copy.wait_send()

    return finish


def scatter_rows_body(axis, count, parts, *refs):
    _, _, _, far, near = level_peers(axis, count)
    greet(far + near)
    start_scatter(axis, count, parts, *refs)()


def scatter_both_body(counts, parts, rows_ref, weight_ref, rows_out, weight_out, *scratch):
    peers = []
    for axis, count in zip(("tensor", "dp"), counts):
        _, _, _, far, near = level_peers(axis, count)
        peers += far + near
    greet(peers)
    second = start_scatter("dp", counts[1], parts[1], weight_ref, weight_out, *scratch[5:])
    first = start_scatter("tensor", counts[0], parts[0], rows_ref, rows_out, *scratch[:5])
    first()
    second()


def scatter_scratch(axis, count, parts, rows, cols):
    outer, inner = split_axis(axis, count)
    return [
        pltpu.VMEM((outer, max(inner - 1, 1), rows, cols), jnp.bfloat16),
        pltpu.VMEM((max(outer - 1, 1), rows, cols), jnp.bfloat16),
        pltpu.VMEM((max(outer - 1, 1), rows, cols), jnp.bfloat16),
        DMA((parts * 2 * count,)),
        DMA((parts * 2 * count,)),
    ]


def scatter_both(values, weight, number):
    counts = (lax.axis_size("tensor"), lax.axis_size("dp"))
    terms = [
        array.reshape(count, array.shape[0] // count, array.shape[1])
        for array, count in zip((values, weight), counts)
    ]
    parts = (parts_of(terms[0].shape[1], 2), parts_of(terms[1].shape[1], 3))
    scratch = []
    for axis, count, part, term in zip(("tensor", "dp"), counts, parts, terms):
        scratch += scatter_scratch(axis, count, part, term.shape[1], term.shape[2])
    return comm_call(
        functools.partial(scatter_both_body, counts, parts),
        [jax.ShapeDtypeStruct(term.shape[1:], jnp.float32) for term in terms],
        scratch,
        number,
        tuple(terms),
    )


def scatter_rows(values, number, axis="tensor", most=2):
    count = lax.axis_size(axis)
    cols = values.shape[1]
    rows = values.shape[0] // count
    parts = parts_of(rows, most)
    return comm_call(
        functools.partial(scatter_rows_body, axis, count, parts),
        jax.ShapeDtypeStruct((rows, cols), jnp.float32),
        scatter_scratch(axis, count, parts, rows, cols),
        number,
        (values.reshape(count, rows, cols),),
    )


def axis_peers(group_count, tensor_count):
    group, place = lax.axis_index("dp"), lax.axis_index("tensor")
    others = [(lax.rem(group + step, group_count), place) for step in range(1, group_count)]
    mates = [(group, lax.rem(place + step, tensor_count)) for step in range(1, tensor_count)]
    return group, place, others, mates


def modulation_body(
    group_count,
    tensor_count,
    parts,
    terms_ref,
    weight_ref,
    out_ref,
    full_ref,
    landed_ref,
    send_sem,
    recv_sem,
    send_two,
    recv_two,
    send_bulk,
    recv_bulk,
    local_sem,
):
    group, place, others, mates = axis_peers(group_count, tensor_count)
    greet(others + mates)
    copies = []
    for index, peer in enumerate(others):
        copies.append(
            push(
                terms_ref.at[peer[0]],
                landed_ref.at[index],
                send_sem.at[index],
                recv_sem.at[index],
                peer,
            )
        )
    finish = start_gather(
        "dp", group_count, parts, weight_ref, full_ref, send_bulk, recv_bulk, local_sem
    )
    total = terms_ref[group]
    for index, copy in enumerate(copies):
        copy.wait_recv()
        total = total + landed_ref[index]
    out_ref[place] = total
    spread = []
    for index, peer in enumerate(mates):
        spread.append(
            push(out_ref.at[place], out_ref.at[place], send_two.at[index], recv_two.at[index], peer)
        )
    finish()
    for copy in spread:
        copy.wait_recv()
    for copy in copies + spread:
        copy.wait_send()


def sum_modulation(terms, weight, number):
    group_count, tensor_count = lax.axis_size("dp"), lax.axis_size("tensor")
    _, latents, cols = terms.shape
    rows, width = weight.shape
    parts = parts_of(rows, 3)
    summed, full = comm_call(
        functools.partial(modulation_body, group_count, tensor_count, parts),
        [
            jax.ShapeDtypeStruct((tensor_count, latents, cols), jnp.float32),
            jax.ShapeDtypeStruct((group_count, rows, width), weight.dtype),
        ],
        [
            pltpu.VMEM((max(group_count - 1, 1), latents, cols), jnp.float32),
            DMA((group_count,)),
            DMA((group_count,)),
            DMA((tensor_count,)),
            DMA((tensor_count,)),
            DMA((parts * group_count,)),
            DMA((parts * group_count,)),
            DMA,
        ],
        number,
        (terms, weight),
    )
    return summed, full.reshape(group_count * rows, width)


def collect_body(
    group_count,
    tensor_count,
    split_ref,
    own_ref,
    split_out,
    own_out,
    landed_ref,
    send_sem,
    recv_sem,
    send_two,
    recv_two,
):
    group, place, others, mates = axis_peers(group_count, tensor_count)
    greet(others + mates)
    copies = []
    for index, peer in enumerate(others):
        copies.append(
            push(own_ref, own_out.at[group], send_two.at[index], recv_two.at[index], peer)
        )
    first = []
    for index, peer in enumerate(mates):
        first.append(
            push(
                split_ref.at[peer[1]],
                landed_ref.at[index],
                send_sem.at[index],
                recv_sem.at[index],
                peer,
            )
        )
    own_out[group] = own_ref[...]
    total = split_ref[place]
    for index, copy in enumerate(first):
        copy.wait_recv()
        total = total + landed_ref[index]
    split_out[group] = total
    count = len(others)
    for index, peer in enumerate(others):
        copies.append(
            push(
                split_out.at[group],
                split_out.at[group],
                send_two.at[count + index],
                recv_two.at[count + index],
                peer,
            )
        )
    for copy in copies:
        copy.wait_recv()
    for copy in copies + first:
        copy.wait_send()


def collect(split, own, number):
    group_count, tensor_count = lax.axis_size("dp"), lax.axis_size("tensor")
    wide, narrow = split.shape[2], own.shape[1]
    return comm_call(
        functools.partial(collect_body, group_count, tensor_count),
        [
            jax.ShapeDtypeStruct((group_count, 1, wide), jnp.float32),
            jax.ShapeDtypeStruct((group_count, 1, narrow), jnp.float32),
        ],
        [
            pltpu.VMEM((max(tensor_count - 1, 1), 1, wide), jnp.float32),
            DMA((tensor_count,)),
            DMA((tensor_count,)),
            DMA((2 * group_count,)),
            DMA((2 * group_count,)),
        ],
        number,
        (split, own),
    )


def spread_body(group_count, tensor_count, one_ref, two_ref, one_out, two_out, send_sem, recv_sem):
    group, place, others, mates = axis_peers(group_count, tensor_count)
    greet(mates)
    copies = []
    count = len(mates)
    for index, peer in enumerate(mates):
        copies.append(
            push(one_ref, one_out.at[place], send_sem.at[index], recv_sem.at[index], peer)
        )
        copies.append(
            push(
                two_ref,
                two_out.at[place],
                send_sem.at[count + index],
                recv_sem.at[count + index],
                peer,
            )
        )
    one_out[place] = one_ref[...]
    two_out[place] = two_ref[...]
    for copy in copies:
        copy.wait_recv()
    for copy in copies:
        copy.wait_send()


def spread_pair(one, two, number):
    group_count, tensor_count = lax.axis_size("dp"), lax.axis_size("tensor")
    return comm_call(
        functools.partial(spread_body, group_count, tensor_count),
        [
            jax.ShapeDtypeStruct((tensor_count,) + one.shape, jnp.float32),
            jax.ShapeDtypeStruct((tensor_count,) + two.shape, jnp.float32),
        ],
        [DMA((2 * tensor_count,)), DMA((2 * tensor_count,))],
        number,
        (one, two),
    )


def gather_weight(weight):
    return lax.all_gather(weight, "dp", axis=0, tiled=True)


def scatter_weight(grad):
    return lax.psum_scatter(grad, "dp", scatter_dimension=0, tiled=True).astype(jnp.float32)


def dot_low(left, right, left_dim, right_dim):
    return lax.dot_general(
        left, right, (((left_dim,), (right_dim,)), ((), ())), preferred_element_type=jnp.float32
    )


def split_heads(values, latent_count):
    return values.reshape(latent_count, SEQ, -1, HEAD_DIM)


def local(
    tokens,
    timesteps,
    labels,
    time_weight,
    class_table,
    mod_weight,
    mod_bias,
    qkv_weight,
    qv_bias,
    proj_weight,
    proj_bias,
    up_weight,
    up_bias,
    down_weight,
    down_bias,
    grad_output,
):
    rows_own, model_width = tokens.shape
    tensor_count = lax.axis_size("tensor")
    group_count = lax.axis_size("dp")
    tensor_place = lax.axis_index("tensor")
    group_rows = rows_own * tensor_count
    latent_count = group_rows // SEQ
    head_cols = qkv_weight.shape[3]
    unit_cols = up_weight.shape[2]
    mod_cols = mod_weight.shape[2]
    own_rows = qkv_weight.shape[2]
    head_start = tensor_place * head_cols
    unit_start = tensor_place * unit_cols
    score_scale = 1.0 / math.sqrt(HEAD_DIM)

    attn_own = jnp.concatenate(
        [qkv_weight[0, 0], qkv_weight[0, 1], qkv_weight[0, 2], proj_weight[0].T], axis=1
    )
    features = time_features(timesteps, time_weight.shape[0])
    one_hot = (
        labels[:, None] == jnp.arange(class_table.shape[0], dtype=jnp.int32)[None, :]
    ).astype(jnp.float32)
    condition = jnp.dot(features, time_weight, precision=PRECISE) + jnp.dot(
        one_hot, class_table, precision=PRECISE
    )
    cond_act = jax.nn.silu(condition).astype(jnp.bfloat16)
    mod_terms = jnp.dot(cond_act, mod_weight[0], preferred_element_type=jnp.float32)
    mod_sum, attn_full = sum_modulation(
        mod_terms.reshape(group_count, latent_count, mod_cols), attn_own, 1
    )
    up_own, down_own, mod_sum = lax.optimization_barrier(
        (up_weight[0], down_weight[0].T, mod_sum)
    )
    down_cut = (unit_cols // 2 + 127) // 128 * 128 if unit_cols > 256 else unit_cols // 2
    up_full = gather_weight(up_own)
    down_left = gather_weight(down_own[:, :down_cut])
    qkv_full = attn_full[:, : 3 * head_cols]
    proj_full = attn_full[:, 3 * head_cols :]
    modulation = mod_sum.transpose(1, 0, 2).reshape(latent_count, -1) + mod_bias

    if SEQ % rows_own == 0:
        my_latent = (tensor_place * rows_own) // SEQ
        rows_mod = lax.dynamic_slice_in_dim(modulation, my_latent, 1, 0)
        mine = (jnp.arange(latent_count, dtype=jnp.int32) == my_latent)[:, None]

        def per_latent(values):
            return jnp.where(mine, jnp.sum(values, axis=0)[None, :], 0.0)

    else:
        row_latent = (tensor_place * rows_own + jnp.arange(rows_own, dtype=jnp.int32)) // SEQ
        selector = (
            row_latent[:, None] == jnp.arange(latent_count, dtype=jnp.int32)[None, :]
        ).astype(jnp.float32)
        rows_mod = jnp.dot(selector, modulation, precision=PRECISE)

        def per_latent(values):
            return jnp.dot(selector.T, values, precision=PRECISE)

    shift_attn, scale_attn, gate_attn, shift_mlp, scale_mlp, gate_mlp = [
        rows_mod[:, segment * model_width : (segment + 1) * model_width] for segment in range(6)
    ]

    def attention_scores(queries, key_rows):
        return (
            jnp.einsum(
                "bqhd,bkhd->bhqk",
                split_heads(queries, latent_count),
                split_heads(key_rows, latent_count),
                preferred_element_type=jnp.float32,
            )
            * score_scale
        )

    bias_query = lax.dynamic_slice_in_dim(qv_bias[0, 0], head_start, head_cols, 0)
    bias_value = lax.dynamic_slice_in_dim(qv_bias[0, 1], head_start, head_cols, 0)
    unit_bias = lax.dynamic_slice_in_dim(up_bias[0], unit_start, unit_cols, 0)
    bias_qkv = jnp.concatenate([bias_query, jnp.zeros_like(bias_query), bias_value])

    normed_attn, inverse_attn = layer_norm(tokens)
    attn_in = gather_rows((normed_attn * (1.0 + scale_attn) + shift_attn).astype(jnp.bfloat16), 2)
    qkv_rows = (dot_low(attn_in, qkv_full, 1, 0) + bias_qkv).astype(jnp.bfloat16)
    queries = qkv_rows[:, :head_cols]
    key_rows = qkv_rows[:, head_cols : 2 * head_cols]
    value_rows = qkv_rows[:, 2 * head_cols :]
    scores = attention_scores(queries, key_rows)
    log_total = jnp.log(jnp.sum(jnp.exp(scores), axis=-1, keepdims=True))
    prob_full = jnp.exp(scores - log_total)
    prob_low = prob_full.astype(jnp.bfloat16)
    attended = (
        jnp.einsum(
            "bhqk,bkhd->bqhd",
            prob_low,
            split_heads(value_rows, latent_count),
            preferred_element_type=jnp.float32,
        )
        .astype(jnp.bfloat16)
        .reshape(group_rows, head_cols)
    )
    attn_out = (
        scatter_rows(dot_low(attended, proj_full, 1, 1).astype(jnp.bfloat16), 3) + proj_bias[0]
    )
    middle = tokens + gate_attn * attn_out
    normed_mlp, inverse_mlp = layer_norm(middle)
    mlp_in = gather_rows((normed_mlp * (1.0 + scale_mlp) + shift_mlp).astype(jnp.bfloat16), 4)
    pre_act = dot_low(mlp_in, up_full, 1, 0) + unit_bias
    gelu_low = gelu_value(pre_act).astype(jnp.bfloat16)
    d_mlp = grad_output * gate_mlp
    down_bias_part = jnp.sum(d_mlp, axis=0)
    d_mlp_all, down_right = gather_both(d_mlp.astype(jnp.bfloat16), down_own[:, down_cut:], 6)
    down_full = jnp.concatenate([down_left, down_right], axis=1)
    grad_down_low = dot_low(d_mlp_all, gelu_low, 0, 0).astype(jnp.bfloat16)
    grad_down_low, gelu_low = lax.optimization_barrier((grad_down_low, gelu_low))
    grad_down = scatter_weight(grad_down_low)
    mlp_out = (
        scatter_rows(dot_low(gelu_low, down_full, 1, 1).astype(jnp.bfloat16), 5) + down_bias[0]
    )
    output = middle + gate_mlp * mlp_out

    d_gate_mlp = per_latent(grad_output * mlp_out)
    d_gelu = dot_low(d_mlp_all, down_full, 1, 0)
    d_pre = d_gelu * gelu_slope(pre_act)
    unit_part = jnp.sum(d_pre, axis=0)
    d_pre_low = d_pre.astype(jnp.bfloat16)
    grad_up_low = dot_low(mlp_in, d_pre_low, 0, 0).astype(jnp.bfloat16)
    grad_up_low, d_pre_low = lax.optimization_barrier((grad_up_low, d_pre_low))
    grad_up = scatter_weight(grad_up_low)
    d_mlp_in = scatter_rows(dot_low(d_pre_low, up_full, 1, 1).astype(jnp.bfloat16), 7)
    d_shift_mlp = per_latent(d_mlp_in)
    d_scale_mlp = per_latent(d_mlp_in * normed_mlp)
    d_middle = grad_output + norm_back(normed_mlp, inverse_mlp, d_mlp_in * (1.0 + scale_mlp))
    d_attn = d_middle * gate_attn
    d_gate_attn = per_latent(d_middle * attn_out)
    proj_bias_part = jnp.sum(d_attn, axis=0)
    d_attn_all = gather_rows(d_attn.astype(jnp.bfloat16), 8)
    d_attended = dot_low(d_attn_all, proj_full, 1, 0).astype(jnp.bfloat16)
    d_heads = split_heads(d_attended, latent_count)
    grad_value = jnp.einsum(
        "bhqk,bqhd->bkhd", prob_low, d_heads, preferred_element_type=jnp.float32
    ).reshape(group_rows, head_cols)
    d_prob = jnp.einsum(
        "bqhd,bkhd->bhqk",
        d_heads,
        split_heads(value_rows, latent_count),
        preferred_element_type=jnp.float32,
    )
    row_delta = jnp.einsum(
        "bqhd,bqhd->bhq",
        d_heads,
        split_heads(attended, latent_count),
        preferred_element_type=jnp.float32,
    )
    d_score_low = (prob_full * (d_prob - row_delta[..., None])).astype(jnp.bfloat16)
    grad_query = (
        jnp.einsum(
            "bhqk,bkhd->bqhd",
            d_score_low,
            split_heads(key_rows, latent_count),
            preferred_element_type=jnp.float32,
        ).reshape(group_rows, head_cols)
        * score_scale
    )
    grad_key = (
        jnp.einsum(
            "bhqk,bqhd->bkhd",
            d_score_low,
            split_heads(queries, latent_count),
            preferred_element_type=jnp.float32,
        ).reshape(group_rows, head_cols)
        * score_scale
    )
    qv_part = jnp.concatenate([jnp.sum(grad_query, axis=0), jnp.sum(grad_value, axis=0)])
    low_rows = jnp.concatenate(
        [
            grad_query.astype(jnp.bfloat16),
            grad_key.astype(jnp.bfloat16),
            grad_value.astype(jnp.bfloat16),
        ],
        axis=1,
    )
    grad_attn_low = jnp.concatenate(
        [
            dot_low(attn_in, low_rows, 0, 0).astype(jnp.bfloat16),
            dot_low(d_attn_all, attended, 0, 0).astype(jnp.bfloat16),
        ],
        axis=1,
    )
    d_attn_in, grad_attn = scatter_both(
        dot_low(low_rows, qkv_full, 1, 1).astype(jnp.bfloat16), grad_attn_low, 9
    )
    d_shift_attn = per_latent(d_attn_in)
    d_scale_attn = per_latent(d_attn_in * normed_attn)
    grad_tokens = d_middle + norm_back(normed_attn, inverse_attn, d_attn_in * (1.0 + scale_attn))

    d_mod_part = jnp.concatenate(
        [d_shift_attn, d_scale_attn, d_gate_attn, d_shift_mlp, d_scale_mlp, d_gate_mlp], axis=1
    )
    bias_cols = model_width // tensor_count
    split = jnp.concatenate(
        [
            d_mod_part[latent].reshape(tensor_count, 1, mod_cols)
            for latent in range(latent_count)
        ]
        + [
            proj_bias_part.reshape(tensor_count, 1, bias_cols),
            down_bias_part.reshape(tensor_count, 1, bias_cols),
        ],
        axis=2,
    )
    own = jnp.concatenate([unit_part, qv_part])[None, :]
    split_all, own_all = collect(split, own, 10)
    mod_end = latent_count * mod_cols
    d_mod_all = split_all[:, 0, :mod_end].reshape(group_count * latent_count, mod_cols)
    totals = jnp.concatenate(
        [
            jnp.sum(d_mod_all, axis=0),
            jnp.sum(split_all[:, 0, mod_end:], axis=0),
            jnp.sum(own_all[:, 0], axis=0),
        ]
    )[None, :]
    cond_wide = cond_act.astype(jnp.float32)
    grad_mod_weight = jnp.dot(cond_wide.T, d_mod_all, precision=PRECISE)[None]
    cond_back = jnp.dot(d_mod_all, mod_weight[0].astype(jnp.float32).T, precision=PRECISE)
    cond_parts, total_parts = spread_pair(cond_back, totals, 11)
    total_parts = total_parts[:, 0]
    ends = [mod_cols, bias_cols, bias_cols, unit_cols, head_cols, head_cols]
    pieces = []
    start = 0
    for width in ends:
        pieces.append(total_parts[:, start : start + width].reshape(1, -1))
        start += width
    modb_total, proj_total, down_total, unit_total, query_total, value_total = pieces
    d_condition = jnp.sum(cond_parts, axis=0) * silu_slope(condition)
    grad_time_weight = jnp.dot(features.T, d_condition, precision=PRECISE)
    grad_class_table = jnp.dot(one_hot.T, d_condition, precision=PRECISE)
    grad_qkv = grad_attn[:, : 3 * head_cols].reshape(own_rows, 3, head_cols).transpose(1, 0, 2)
    return (
        output,
        grad_tokens,
        grad_time_weight,
        grad_class_table,
        grad_mod_weight,
        modb_total,
        grad_qkv[None],
        jnp.concatenate([query_total, value_total])[None],
        grad_attn[:, 3 * head_cols :].T[None],
        proj_total,
        grad_up[None],
        unit_total,
        grad_down.T[None],
        down_total,
    )


def solution(mesh):
    in_specs = (
        P(("dp", "tensor"), None),
        P(),
        P(),
        P(None, "dp"),
        P(None, "dp"),
        P(None, "dp", "tensor"),
        P(),
        P(None, None, "dp", "tensor"),
        P(),
        P(None, "tensor", "dp"),
        P(),
        P(None, "dp", "tensor"),
        P(),
        P(None, "tensor", "dp"),
        P(),
        P(("dp", "tensor"), None),
    )
    out_specs = (
        P(("dp", "tensor"), None),
        P(("dp", "tensor"), None),
        P(None, "dp"),
        P(None, "dp"),
        P(None, "dp", "tensor"),
        P(),
        P(None, None, "dp", "tensor"),
        P(),
        P(None, "tensor", "dp"),
        P(),
        P(None, "dp", "tensor"),
        P(),
        P(None, "tensor", "dp"),
        P(),
    )
    return jax.shard_map(local, mesh=mesh, in_specs=in_specs, out_specs=out_specs, check_vma=False)
```
